128 devices in a mesh: row: 16 (over y, z), col: 8 (over x, core).
Axes of the slice: x: 4, y: 4, z: 4, core: 2. Of those that a mesh axis runs over, the one named last changes fastest.
Arguments:
- front: float32 [2, 8192, 4, 4096], P(None, 'row', None, 'col')
- child_blocks: float32 [2, 8192, 8192], P(None, 'row', 'col')
- index_maps: int32 [2, 8192], replicated, may hold values from 0 to 16383, as said below
Outputs:
- schur: float32 [2, 8192, 4, 4096], P(None, 'row', None, 'col')
- factor: float32 [2, 8192, 1024], P(None, 'row')
The draws below stay inside these ranges and needn't reach their ends.
Inputs may be any that keep to these rules, and one draw needn't show every extreme that they name: Within one child the map names distinct front indices. Entry index_maps[h, (s * R + k) * 32 + i], with R the number of row indices, names an index in a block b of 512 indices with b mod R equal to k.
All inputs are finite; a program needn't handle non-finite values.
Results may differ from the reference program's by a relative error of at most 0.0001.
Values sent between devices are 32-bit elements; how exact they have to be, the bound alone decides.
A program may use at most 128 MiB of HBM per device.

```python
import math
import jax
import jax.numpy as jnp
from jax import lax

F = 16384
NB = 512
NCH = 2
CAPR = 32
CH = 8192
N_ROW = 16
N_COL = 8


def lax_iota(shape, dim):
    return jax.lax.broadcasted_iota(jnp.int32, shape, dim)


def symmetric_noise(key, order):
    noise = jnp.clip(0.7 * jax.random.normal(key, (order, order), jnp.float32), -4.2, 4.2)
    upper = lax_iota((order, order), 0) <= lax_iota((order, order), 1)
    return jnp.where(upper, noise, noise.T)


def draw_front(key, part):
    shape = (F // (NB * N_ROW), N_ROW * NB, F // (NB * N_COL), N_COL * NB)
    first, second = jax.random.split(key)
    base = symmetric_noise(first, F)
    diag_vals = jnp.exp(jax.random.uniform(second, (F,), jnp.float32, math.log(96.0), math.log(320.0)))
    same = lax_iota((F, F), 0) == lax_iota((F, F), 1)
    whole = jnp.where(same, diag_vals[None, :], base)
    return whole.reshape(shape)


def draw_child_blocks(key, part):
    keys = jax.random.split(key, NCH)
    return jnp.stack([symmetric_noise(keys[child], CH) for child in range(NCH)], axis=0)


def owner_maps(key, count, slots):
    owned = F // count
    subkeys = jax.random.split(key, NCH * count)
    chosen = jax.vmap(lambda subkey: jax.random.permutation(subkey, owned)[:count * slots])(subkeys).astype(jnp.int32)
    owner = (jnp.arange(NCH * count, dtype=jnp.int32) % count)[:, None]
    whole = chosen // NB * (NB * count) + owner * NB + chosen % NB
    whole = whole.reshape(NCH, count, count, slots).transpose(0, 2, 1, 3)
    return whole.reshape(NCH, count * count * slots).astype(jnp.int32)


def draw_index_maps(key, part):
    return owner_maps(key, N_ROW, CAPR)


def setup_inputs(seed: int = 0) -> dict:
    key_list = jax.random.split(jax.random.key(seed), 4)
    front = draw_front(jax.random.fold_in(key_list[3], 71), 0)
    child_blocks = draw_child_blocks(jax.random.fold_in(key_list[3], 71), 0)
    index_maps = draw_index_maps(jax.random.fold_in(key_list[3], 71), 0)
    return dict(front=front, child_blocks=child_blocks, index_maps=index_maps)


def reference(front, child_blocks, index_maps):
    summed = front.reshape(F, F)
    for child in range(NCH):
        mapping = index_maps[child]
        summed = summed.at[mapping[:, None], mapping[None, :]].add(child_blocks[child])
    panels = []
    for section in range(2):
        start = section * NB
        block = summed[start:start + NB, start:start + NB]
        lower = jnp.linalg.cholesky(block)
        column = summed[:, start:start + NB]
        solved = lax.linalg.triangular_solve(lower, column, left_side=False, lower=True, transpose_a=True)
        solved = solved.at[start:start + NB].set(lower)
        solved = solved.at[:start].set(jnp.zeros((start, NB), jnp.float32))
        summed = summed - jnp.dot(solved.astype(jnp.float32), solved.T.astype(jnp.float32), precision=lax.Precision.HIGHEST, preferred_element_type=jnp.float32)
        panels.append(solved)
    schur = summed.reshape(front.shape)
    factor = jnp.concatenate(panels, axis=1).reshape(F // (NB * N_ROW), N_ROW * NB, 2 * NB)
    return (schur, factor)
```

```python
import functools
import jax
import jax.numpy as jnp
from jax import lax
from jax.experimental import pallas as pl
from jax.experimental.pallas import tpu as pltpu
from jax.sharding import PartitionSpec as P

NB = 512
MESH = pl.DeviceIdType.MESH
BF = jnp.bfloat16
F32 = jnp.float32


def split3(value):
    first = value.astype(BF)
    rest = value - first.astype(F32)
    second = rest.astype(BF)
    third = (rest - second.astype(F32)).astype(BF)
    return first, second, third


def dot(left, right):
    return jnp.dot(left, right, preferred_element_type=F32)


def exchange_kernel(rows, cols, child_ref, front_ref, row_ids_ref, col_ids_ref, out_ref,
                    staged, grouped, received, summed, child_sem, front_sems, send_sems, recv_sem):
    my_row = lax.axis_index("row")
    my_col = lax.axis_index("col")
    loads = [
        pltpu.make_async_copy(child_ref, staged, child_sem)
    ]
    loads[0].start()
    for b in range(2):
        for q in range(4):
            pltpu.make_async_copy(
                front_ref.at[b, :, q, :],
                summed.at[pl.ds(b * NB, NB), pl.ds(q * NB, NB)],
                front_sems.at[b * 4 + q],
            ).start()
    loads[0].wait()

    def group_rows(k):
        lanes = lax.broadcasted_iota(jnp.int32, (32, 128), 1) // 32
        at = pl.ds(pl.multiple_of(k * 32, 32), 32)
        for h in range(2):
            tiles = [staged[h, at, t * 128:(t + 1) * 128] for t in range(8)]
            for dest in range(8):
                made = None
                for part in range(4):
                    source = tiles[part * 2 + dest // 4]
                    shift = (part * 32 - (dest % 4) * 32) % 128
                    moved = pltpu.roll(source, shift, axis=1) if shift else source
                    made = moved if made is None else jnp.where(lanes == part, moved, made)
                grouped[h, at, dest * 128:(dest + 1) * 128] = made

    def block(ref, row, col):
        return ref.at[
            :, pl.ds(pl.multiple_of(row * 32, 32), 32), pl.ds(pl.multiple_of(col * 128, 128), 128)
        ]

    def send(k, dest, sem):
        pltpu.make_async_remote_copy(
            src_ref=block(grouped, k, dest),
            dst_ref=block(received, my_row, my_col),
            send_sem=send_sems.at[sem],
            recv_sem=recv_sem,
            device_id=(k, dest),
            device_id_type=MESH,
        ).start()

    @pl.loop(0, rows)
    def _(t):
        k = lax.rem(my_row + t, rows)
        group_rows(k)
        for u in range(1, cols):
            send(k, lax.rem(my_col + u, cols), 0)

        @pl.when(t > 0)
        def _():
            send(k, my_col, 1)

    own = pltpu.make_async_copy(
        block(grouped, my_row, my_col), block(received, my_row, my_col), recv_sem
    )
    own.start()
    for b in range(2):
        for q in range(4):
            pltpu.make_async_copy(
                front_ref.at[b, :, q, :],
                summed.at[pl.ds(b * NB, NB), pl.ds(q * NB, NB)],
                front_sems.at[b * 4 + q],
            ).wait()
    pltpu.make_async_copy(received, received, recv_sem).wait()
    pltpu.make_async_copy(
        grouped.at[:, :, pl.ds(0, 896)], grouped.at[:, :, pl.ds(0, 896)], send_sems.at[0]
    ).wait()
    pltpu.make_async_copy(
        grouped.at[:, pl.ds(0, 480), pl.ds(0, 128)],
        grouped.at[:, pl.ds(0, 480), pl.ds(0, 128)],
        send_sems.at[1],
    ).wait()

    for h in range(2):
        pieces = [split3(received[h, r:r + 256, :]) for r in (0, 256)]
        stacked = jnp.concatenate([p for piece in pieces for p in piece], axis=0)
        row_map = (
            lax.broadcasted_iota(jnp.int32, (1024, 512), 0) == row_ids_ref[h:h + 1, :]
        ).astype(BF)

        @pl.loop(0, 8)
        def _(n):
            at = pl.ds(pl.multiple_of(n * 256, 256), 256)
            col_map = (
                lax.broadcasted_iota(jnp.int32, (1024, 256), 1) + n * 256 == col_ids_ref[h]
            ).astype(BF)
            wide = dot(stacked, col_map)
            total = summed[:, at]
            for half in range(2):
                base = half * 768
                value = (wide[base:base + 256] + wide[base + 256:base + 512]) + wide[base + 512:base + 768]
                for p in split3(value):
                    total += dot(row_map[:, half * 256:half * 256 + 256], p)
            summed[:, at] = total

    done = pltpu.make_async_copy(summed, out_ref, child_sem)
    done.start()
    done.wait()


def local_position(ids, count):
    return ids // (NB * count) * NB + ids % NB


def id_tables(index_maps, rows, cols):
    my_row = lax.axis_index("row")
    my_col = lax.axis_index("col")
    ratio = rows // cols
    row_ids = lax.dynamic_index_in_dim(
        index_maps.reshape(2, rows, rows, -1), my_row, 2, keepdims=False
    ).reshape(2, -1)
    col_ids = lax.dynamic_index_in_dim(
        index_maps.reshape(2, cols, ratio, ratio, cols, -1), my_col, 4, keepdims=False
    ).reshape(2, -1)
    return local_position(row_ids, rows), local_position(col_ids, cols)[:, :, None]


def exchange(front, child_blocks, index_maps, rows, cols):
    row_ids, col_ids = id_tables(index_maps, rows, cols)
    vm = pl.BlockSpec(memory_space=pltpu.VMEM)
    anyspace = pl.BlockSpec(memory_space=pl.ANY)
    return pl.pallas_call(
        functools.partial(exchange_kernel, rows, cols),
        out_shape=jax.ShapeDtypeStruct((1024, 2048), F32),
        in_specs=[anyspace, anyspace, vm, vm],
        out_specs=anyspace,
        scratch_shapes=[
            pltpu.VMEM((2, 512, 1024), F32),
            pltpu.VMEM((2, 512, 1024), F32),
            pltpu.VMEM((2, 512, 1024), F32),
            pltpu.VMEM((1024, 2048), F32),
            pltpu.SemaphoreType.DMA,
            pltpu.SemaphoreType.DMA((8,)),
            pltpu.SemaphoreType.DMA((2,)),
            pltpu.SemaphoreType.DMA,
        ],
        compiler_params=pltpu.CompilerParams(vmem_limit_bytes=60 << 20, has_side_effects=True),
    )(child_blocks, front, row_ids, col_ids)


def spread(value, axis, source):
    kept = jnp.where(lax.axis_index(axis) == source, value, 0).astype(value.dtype)
    return lax.psum(kept, axis)


def share_panel(values, root):
    return spread(values, "col", root)


def factor_panel(panel, section, my_row, row_count):
    pivot = spread(panel[:NB], "row", section)
    lower = jnp.linalg.cholesky(pivot)
    solved = lax.linalg.triangular_solve(
        lower, panel, left_side=False, lower=True, transpose_a=True
    )
    rows_local = panel.shape[0]
    block_ids = jnp.arange(rows_local, dtype=jnp.int32) // NB * row_count + my_row
    tiled = jnp.tile(lower, (rows_local // NB, 1))
    zeros = jnp.zeros_like(solved)
    picked = jnp.where((block_ids == section)[:, None], tiled, solved)
    return jnp.where((block_ids < section)[:, None], zeros, picked)


def column_rows(factor_rows, my_col, row_count, col_count):
    pieces = [
        spread(factor_rows, "row", my_col + turn * col_count)
        for turn in range(row_count // col_count)
    ]
    blocks = factor_rows.shape[0] // NB
    shaped = [piece.reshape(blocks, NB, NB) for piece in pieces]
    return jnp.stack(shaped, axis=1).reshape(-1, NB)


def outer_update(matrix, left_rows, right_rows):
    return matrix - jnp.dot(
        left_rows, right_rows.T, precision=lax.Precision.HIGHEST, preferred_element_type=jnp.float32
    )


def on_device(front, child_blocks, index_maps):
    row_blocks, block_rows, col_blocks, block_cols = front.shape
    row_count = lax.axis_size("row")
    col_count = lax.axis_size("col")
    my_row = lax.axis_index("row")
    my_col = lax.axis_index("col")
    summed = exchange(front, child_blocks, index_maps, row_count, col_count)
    panel = share_panel(summed[:, :NB], 0)
    outputs = []
    for section in range(2):
        factor_rows = factor_panel(panel, section, my_row, row_count)
        factor_cols = column_rows(factor_rows, my_col, row_count, col_count)
        summed = outer_update(summed, factor_rows, factor_cols)
        outputs.append(factor_rows)
        if section == 0:
            panel = share_panel(summed[:, :NB], 1)
    schur = summed.reshape(front.shape)
    factor = jnp.concatenate(outputs, axis=1).reshape(row_blocks, block_rows, 2 * NB)
    return (schur, factor)


def solution(mesh):
    placed = (P(None, "row", None, "col"), P(None, "row", "col"), P())
    return jax.shard_map(
        on_device,
        mesh=mesh,
        in_specs=placed,
        out_specs=(P(None, "row", None, "col"), P(None, "row", None)),
        check_vma=False,
    )
```

```python
import functools

import jax
import jax.numpy as jnp
from jax import lax
from jax.experimental import pallas as pl
from jax.experimental.pallas import tpu as pltpu
from jax.sharding import PartitionSpec as P

NB = 512
MESH = pl.DeviceIdType.MESH
BF = jnp.bfloat16
F32 = jnp.float32
VM = pltpu.VMEM
HI = lax.Precision.HIGHEST


def split3(value):
    first = value.astype(BF)
    rest = value - first.astype(F32)
    second = rest.astype(BF)
    third = (rest - second.astype(F32)).astype(BF)
    return first, second, third


def dot(left, right):
    return jnp.dot(left, right, preferred_element_type=F32)


def exchange_kernel(rows, cols, child_ref, front_ref, row_ids_ref, col_ids_ref, out_ref,
                    staged, grouped, received, summed, child_sem, front_sems, send_sems, recv_sem):
    my_row = lax.axis_index("row")
    my_col = lax.axis_index("col")
    loads = [
        pltpu.make_async_copy(child_ref, staged, child_sem)
    ]
    loads[0].start()
    for b in range(2):
        for q in range(4):
            pltpu.make_async_copy(
                front_ref.at[b, :, q, :],
                summed.at[pl.ds(b * NB, NB), pl.ds(q * NB, NB)],
                front_sems.at[b * 4 + q],
            ).start()
    loads[0].wait()

    def group_rows(k):
        lanes = lax.broadcasted_iota(jnp.int32, (32, 128), 1) // 32
        at = pl.ds(pl.multiple_of(k * 32, 32), 32)
        for h in range(2):
            tiles = [staged[h, at, t * 128:(t + 1) * 128] for t in range(8)]
            for dest in range(8):
                made = None
                for part in range(4):
                    source = tiles[part * 2 + dest // 4]
                    shift = (part * 32 - (dest % 4) * 32) % 128
                    moved = pltpu.roll(source, shift, axis=1) if shift else source
                    made = moved if made is None else jnp.where(lanes == part, moved, made)
                grouped[h, at, dest * 128:(dest + 1) * 128] = made

    def block(ref, row, col):
        return ref.at[
            :, pl.ds(pl.multiple_of(row * 32, 32), 32), pl.ds(pl.multiple_of(col * 128, 128), 128)
        ]

    def send(k, dest, sem):
        pltpu.make_async_remote_copy(
            src_ref=block(grouped, k, dest),
            dst_ref=block(received, my_row, my_col),
            send_sem=send_sems.at[sem],
            recv_sem=recv_sem,
            device_id=(k, dest),
            device_id_type=MESH,
        ).start()

    @pl.loop(0, rows)
    def _(t):
        k = lax.rem(my_row + t, rows)
        group_rows(k)
        for u in range(1, cols):
            send(k, lax.rem(my_col + u, cols), 0)

        @pl.when(t > 0)
        def _():
            send(k, my_col, 1)

    own = pltpu.make_async_copy(
        block(grouped, my_row, my_col), block(received, my_row, my_col), recv_sem
    )
    own.start()
    for b in range(2):
        for q in range(4):
            pltpu.make_async_copy(
                front_ref.at[b, :, q, :],
                summed.at[pl.ds(b * NB, NB), pl.ds(q * NB, NB)],
                front_sems.at[b * 4 + q],
            ).wait()
    pltpu.make_async_copy(received, received, recv_sem).wait()
    pltpu.make_async_copy(
        grouped.at[:, :, pl.ds(0, 896)], grouped.at[:, :, pl.ds(0, 896)], send_sems.at[0]
    ).wait()
    pltpu.make_async_copy(
        grouped.at[:, pl.ds(0, 480), pl.ds(0, 128)],
        grouped.at[:, pl.ds(0, 480), pl.ds(0, 128)],
        send_sems.at[1],
    ).wait()

    for h in range(2):
        pieces = [split3(received[h, r:r + 256, :]) for r in (0, 256)]
        stacked = jnp.concatenate([p for piece in pieces for p in piece], axis=0)
        row_map = (
            lax.broadcasted_iota(jnp.int32, (1024, 512), 0) == row_ids_ref[h:h + 1, :]
        ).astype(BF)

        @pl.loop(0, 8)
        def _(n):
            at = pl.ds(pl.multiple_of(n * 256, 256), 256)
            col_map = (
                lax.broadcasted_iota(jnp.int32, (1024, 256), 1) + n * 256 == col_ids_ref[h]
            ).astype(BF)
            wide = dot(stacked, col_map)
            total = summed[:, at]
            for half in range(2):
                base = half * 768
                value = (wide[base:base + 256] + wide[base + 256:base + 512]) + wide[base + 512:base + 768]
                for p in split3(value):
                    total += dot(row_map[:, half * 256:half * 256 + 256], p)
            summed[:, at] = total

    done = pltpu.make_async_copy(summed, out_ref, child_sem)
    done.start()
    done.wait()


def local_position(ids, count):
    return ids // (NB * count) * NB + ids % NB


def id_tables(index_maps, rows, cols):
    my_row = lax.axis_index("row")
    my_col = lax.axis_index("col")
    ratio = rows // cols
    row_ids = lax.dynamic_index_in_dim(
        index_maps.reshape(2, rows, rows, -1), my_row, 2, keepdims=False
    ).reshape(2, -1)
    col_ids = lax.dynamic_index_in_dim(
        index_maps.reshape(2, cols, ratio, ratio, cols, -1), my_col, 4, keepdims=False
    ).reshape(2, -1)
    return local_position(row_ids, rows), local_position(col_ids, cols)[:, :, None]


def exchange(front, child_blocks, index_maps, rows, cols):
    row_ids, col_ids = id_tables(index_maps, rows, cols)
    vm = pl.BlockSpec(memory_space=pltpu.VMEM)
    anyspace = pl.BlockSpec(memory_space=pl.ANY)
    return pl.pallas_call(
        functools.partial(exchange_kernel, rows, cols),
        out_shape=jax.ShapeDtypeStruct((1024, 2048), F32),
        in_specs=[anyspace, anyspace, vm, vm],
        out_specs=anyspace,
        scratch_shapes=[
            pltpu.VMEM((2, 512, 1024), F32),
            pltpu.VMEM((2, 512, 1024), F32),
            pltpu.VMEM((2, 512, 1024), F32),
            pltpu.VMEM((1024, 2048), F32),
            pltpu.SemaphoreType.DMA,
            pltpu.SemaphoreType.DMA((8,)),
            pltpu.SemaphoreType.DMA((2,)),
            pltpu.SemaphoreType.DMA,
        ],
        compiler_params=pltpu.CompilerParams(vmem_limit_bytes=60 << 20, has_side_effects=True),
    )(child_blocks, front, row_ids, col_ids)


def dot_nn(a,b): return lax.dot_general(a,b,(((1,),(0,)),((),())),precision=HI,preferred_element_type=F32)
def dot_nt(a,b): return lax.dot_general(a,b,(((1,),(1,)),((),())),precision=HI,preferred_element_type=F32)

def inverse_factor(block):
    n = 128
    lane = lax.broadcasted_iota(jnp.int32, (8, n), 1)
    sub = lax.broadcasted_iota(jnp.int32, (8, n), 0)
    tiles = [block[8 * i:8 * i + 8, :] for i in range(n // 8)]
    for j in range(n):
        at, inner = j // 8, j % 8
        row = tiles[at][inner:inner + 1, :]
        pivot = row[:, j:j + 1]
        scaled = jnp.where(lane[:1] == j, 1.0, row) / pivot
        for i in range(at, n // 8):
            column = tiles[i][:, j:j + 1]
            if i == at:
                if inner == 7:
                    continue
                below = sub > inner
                update = jnp.where(lane == j, 0.0, tiles[i]) - column * scaled
                tiles[i] = jnp.where(below, update, tiles[i])
            else:
                tiles[i] = jnp.where(lane == j, 0.0, tiles[i]) - column * scaled
    whole = jnp.concatenate(tiles, axis=0)
    r = lax.broadcasted_iota(jnp.int32, (n, n), 0)
    c = lax.broadcasted_iota(jnp.int32, (n, n), 1)
    diag = jnp.sum(jnp.where(r == c, whole, 0.0), axis=1, keepdims=True)
    unit = jnp.where(r > c, whole, jnp.where(r == c, 1.0, 0.0))
    return unit * (1.0 / jnp.sqrt(diag))

def factor_leading(lead, lower, inverse, work, corner, between):
    n = 128
    r = lax.broadcasted_iota(jnp.int32, (n, n), 0)
    c = lax.broadcasted_iota(jnp.int32, (n, n), 1)
    work[...] = lead[...]
    lower[...] = jnp.zeros_like(lower)
    inverse[...] = jnp.zeros_like(inverse)

    @pl.loop(0, 8)
    def _(j):
        at = pl.ds(pl.multiple_of(j * n, n), n)
        corner[...] = inverse_factor(work[at, at])
        for s in range(8):
            @pl.when(j == s)
            def _():
                at = slice(s * n, s * n + n)
                w = corner[...]
                lower[at, at] = jnp.where(r >= c, dot_nt(work[at, at], w), 0.0)
                inverse[at, at] = w
                if s < 7:
                    p = dot_nt(work[s * n + n:, at], w)
                    lower[s * n + n:, at] = p
                    for k in range(s + 1, 8):
                        o = (k - s - 1) * n
                        work[k * n:, k * n:k * n + n] -= dot_nt(p[o:], p[o:o + n])
                if s:
                    done = slice(0, s * n)
                    inverse[at, done] = -dot_nn(w, dot_nn(lower[at, done], inverse[done, done]))
                if s in between:
                    between[s]()


def share_kernel(summed_ref, rows_out, cols_out, lower_out, inverse_out,
                 rows_ref, cols_ref, lead_ref, lower, inverse, work, corner, sent, got, out_sems):
    wait_bytes = cols_ref
    my_row = lax.axis_index("row")
    my_col = lax.axis_index("col")
    y, z = my_row // 4, my_row % 4
    x, core = my_col // 2, my_col % 2
    chip = my_row * 4 + x

    def remote(src, dst, phase, row, col, send_phase=None):
        leaving = sent.at[phase if send_phase is None else send_phase]
        pltpu.make_async_remote_copy(
            src_ref=src, dst_ref=dst, send_sem=leaving, recv_sem=got.at[phase],
            device_id=(row, col), device_id_type=MESH,
        ).start()

    def local(src, dst, phase):
        pltpu.make_async_copy(src, dst, got.at[phase]).start()

    def wait(sem, ref):
        pltpu.make_async_copy(ref, ref, sem).wait()

    def rows_of(ref, start, size, cols=None):
        at = pl.ds(pl.multiple_of(start, 8), size)
        if cols is None:
            return ref.at[at]
        return ref.at[at, pl.ds(cols[0], cols[1])]

    def lead_piece(ref, block, m):
        if block == 0:
            return rows_of(ref, m * 8, 8, (0, 512))
        if block == 1:
            return rows_of(ref, 512 + m * 8, 8, (0, 256))
        if block == 2:
            return rows_of(ref, 512 + m * 8, 8, (256, 256))
        return rows_of(ref, 512 + m * 8, 8, (512, 512))

    def summed_piece(block, m):
        if block == 1:
            return rows_of(summed_ref, m * 8, 8, (0, 256))
        if block == 2:
            return rows_of(summed_ref, m * 8, 8, (256, 256))
        return rows_of(summed_ref, m * 8, 8, (0, 512))

    for owner_row, owner_col, blocks in ((0, 0, (0,)), (1, 0, (1, 2)), (1, 1, (3,))):
        @pl.when((my_row == owner_row) & (my_col == owner_col))
        def _():
            for block in blocks:
                target_core = 0 if block < 2 else 1

                @pl.loop(0, 64)
                def _(m):
                    row, col = m // 4, (m % 4) * 2 + target_core
                    here = (row == owner_row) & (col == owner_col)

                    @pl.when(here)
                    def _():
                        local(summed_piece(block, m), lead_piece(lead_ref, block, m), 0)

                    @pl.when(jnp.logical_not(here))
                    def _():
                        remote(
                            summed_piece(block, m), lead_piece(lead_ref, block, m), 0, row, col,
                            11 if block == 2 else 0,
                        )

    for src in range(2):
        @pl.when(my_row == src)
        def _():
            for k in range(16):
                piece = rows_of(summed_ref, k * 32, 32)
                place = rows_of(cols_ref, src * NB + k * 32, 32)
                if k == src:
                    local(piece, place, 1)
                else:
                    remote(piece, place, 1, k, my_col)

    for src in range(2):
        @pl.when(my_col == src)
        def _():
            for k in range(4):
                piece = rows_of(summed_ref, k * 256, 256, (0, 512))
                place = rows_of(rows_ref, k * 256, 256, (src * 512, 512))
                if k == 0:
                    local(piece, place, 2)
                else:
                    remote(piece, place, 2, my_row, 2 * k + src)

    @pl.when(core == 0)
    def _():
        wait(got.at[0], wait_bytes.at[pl.ds(0, 8), pl.ds(0, 768)])

        @pl.loop(1, 64)
        def _(t):
            other = lax.rem(chip + t, 64)
            for block in (0, 1):
                remote(lead_piece(lead_ref, block, chip), lead_piece(lead_ref, block, chip), 3, other // 4, (other % 4) * 2)

    @pl.when(core == 1)
    def _():
        wait(got.at[0], wait_bytes.at[pl.ds(0, 8), pl.ds(0, 768)])

        @pl.loop(1, 64)
        def _(t):
            other = lax.rem(chip + t, 64)
            for block in (2, 3):
                remote(lead_piece(lead_ref, block, chip), lead_piece(lead_ref, block, chip), 3, other // 4, (other % 4) * 2 + 1)

    wait(got.at[2], rows_of(wait_bytes, 0, 256, (0, 512)))
    for core_is in range(2):
        @pl.when(core == core_is)
        def _():
            for t in range(1, 4):
                piece = rows_of(rows_ref, x * 256, 256, (core_is * 512, 512))
                remote(piece, piece, 4, my_row, lax.rem(x + t, 4) * 2 + core_is)

    wait(got.at[1], rows_of(wait_bytes, 0, 64, (0, 2048)))
    for src in range(2):
        left = rows_of(cols_ref, src * NB + my_row * 32, 32, (0, 1024))
        right = rows_of(cols_ref, src * NB + my_row * 32, 32, (1024, 1024))
        for t in range(1, 4):
            remote(left, left, 5, y * 4 + lax.rem(z + t, 4), my_col)
            remote(right, right, 6, lax.rem(y + t, 4) * 4 + z, my_col)

    wait(got.at[3], rows_of(wait_bytes, 0, 504, (0, 768)))
    for core_is in range(2):
        @pl.when(core == core_is)
        def _():
            if core_is == 0:
                pieces = [lead_ref.at[pl.ds(0, 512), pl.ds(0, 512)], lead_ref.at[pl.ds(512, 512), pl.ds(0, 256)]]
            else:
                pieces = [lead_ref.at[pl.ds(512, 512), pl.ds(256, 256)], lead_ref.at[pl.ds(512, 512), pl.ds(512, 512)]]
            for piece in pieces:
                remote(piece, piece, 7, my_row, x * 2 + 1 - core_is)

    def second_step():
        wait(got.at[5], rows_of(wait_bytes, 0, 192, (0, 1024)))
        wait(got.at[6], rows_of(wait_bytes, 0, 192, (0, 1024)))
        for src in range(2):
            left = rows_of(cols_ref, src * NB + y * 128, 128, (0, 1024))
            for t in range(1, 4):
                remote(left, left, 8, lax.rem(y + t, 4) * 4 + z, my_col)
            for k in range(4):
                right = rows_of(cols_ref, src * NB + k * 128 + z * 32, 32, (1024, 1024))
                for t in range(1, 4):
                    remote(right, right, 9, y * 4 + lax.rem(z + t, 4), my_col)

    def other_core():
        wait(got.at[4], rows_of(wait_bytes, 0, 768, (0, 512)))
        for core_is in range(2):
            @pl.when(core == core_is)
            def _():
                piece = rows_ref.at[:, pl.ds(core_is * 512, 512)]
                remote(piece, piece, 10, my_row, x * 2 + 1 - core_is)

    wait(got.at[7], rows_of(wait_bytes, 0, 512, (0, 768)))
    factor_leading(lead_ref, lower, inverse, work, corner, {1: second_step, 3: other_core})
    outs = [
        pltpu.make_async_copy(inverse, inverse_out, out_sems.at[0]),
        pltpu.make_async_copy(rows_ref, rows_out, out_sems.at[1]),
        pltpu.make_async_copy(cols_ref, cols_out, out_sems.at[2]),
    ]
    outs[0].start()
    for src in range(2):
        @pl.when(my_row == src)
        def _():
            pltpu.make_async_copy(lower.at[pl.ds(src * NB, NB)], lower_out, out_sems.at[3]).start()
    wait(got.at[8], rows_of(wait_bytes, 0, 768, (0, 1024)))
    wait(got.at[9], rows_of(wait_bytes, 0, 768, (0, 1024)))
    wait(got.at[10], rows_of(wait_bytes, 0, 1024, (0, 512)))

    outs[1].start()
    outs[2].start()

    @pl.when((my_row == 0) & (my_col == 0))
    def _():
        wait(sent.at[0], rows_of(wait_bytes, 0, 504, (0, 512)))

    @pl.when((my_row == 1) & (my_col == 0))
    def _():
        wait(sent.at[0], rows_of(wait_bytes, 0, 504, (0, 256)))
        wait(sent.at[11], rows_of(wait_bytes, 0, 512, (0, 256)))

    @pl.when((my_row == 1) & (my_col == 1))
    def _():
        wait(sent.at[0], rows_of(wait_bytes, 0, 504, (0, 512)))

    @pl.when(my_row < 2)
    def _():
        wait(sent.at[1], rows_of(wait_bytes, 0, 480, (0, 2048)))

    @pl.when(my_col < 2)
    def _():
        wait(sent.at[2], rows_of(wait_bytes, 0, 768, (0, 512)))

    wait(sent.at[3], rows_of(wait_bytes, 0, 504, (0, 768)))
    wait(sent.at[4], rows_of(wait_bytes, 0, 768, (0, 512)))
    wait(sent.at[5], rows_of(wait_bytes, 0, 192, (0, 1024)))
    wait(sent.at[6], rows_of(wait_bytes, 0, 192, (0, 1024)))
    wait(sent.at[7], rows_of(wait_bytes, 0, 512, (0, 768)))
    wait(sent.at[8], rows_of(wait_bytes, 0, 768, (0, 1024)))
    wait(sent.at[9], rows_of(wait_bytes, 0, 768, (0, 1024)))
    wait(sent.at[10], rows_of(wait_bytes, 0, 1024, (0, 512)))
    for out in outs:
        out.wait()

    @pl.when(my_row < 2)
    def _():
        pltpu.make_async_copy(lower.at[pl.ds(0, NB)], lower_out, out_sems.at[3]).wait()


def share(summed):
    anyspace = pl.BlockSpec(memory_space=pl.ANY)
    return pl.pallas_call(
        share_kernel,
        out_shape=(
            jax.ShapeDtypeStruct((1024, 1024), F32),
            jax.ShapeDtypeStruct((1024, 2048), F32),
            jax.ShapeDtypeStruct((512, 1024), F32),
            jax.ShapeDtypeStruct((1024, 1024), F32),
        ),
        in_specs=[anyspace],
        out_specs=[anyspace] * 4,
        scratch_shapes=[
            VM((1024, 1024), F32),
            VM((1024, 2048), F32),
            VM((1024, 1024), F32),
            VM((1024, 1024), F32),
            VM((1024, 1024), F32),
            VM((1024, 1024), F32),
            VM((128, 128), F32),
            pltpu.SemaphoreType.DMA((12,)),
            pltpu.SemaphoreType.DMA((12,)),
            pltpu.SemaphoreType.DMA((4,)),
        ],
        compiler_params=pltpu.CompilerParams(vmem_limit_bytes=60 << 20, has_side_effects=True),
    )(summed)


def split2(value):
    first = value.astype(BF)
    return first, (value - first.astype(F32)).astype(BF)


def product(left, right, dims):
    parts = [(0, 0), (0, 1), (1, 0)]
    total = None
    for a, b in parts:
        term = lax.dot_general(left[a], right[b], (dims, ((), ())), preferred_element_type=F32)
        total = term if total is None else total + term
    return total


def update_kernel(summed_hbm, rows_hbm, cols_hbm, lower_hbm, inverse_hbm, schur_hbm, factor_hbm,
                  summed, rows, cols, inverse, solved, inv_hi, inv_lo, sol_hi, sol_lo,
                  col_hi, col_lo, y_hi, y_lo, in_sems, strip_sems, out_sems, factor_sems):
    my_row = lax.axis_index("row")
    loads = [
        pltpu.make_async_copy(inverse_hbm, inverse, in_sems.at[0]),
        pltpu.make_async_copy(rows_hbm, rows, in_sems.at[1]),
    ]
    for load in loads:
        load.start()

    def strip_loads(q):
        at = pl.ds(q * NB, NB)
        return [
            pltpu.make_async_copy(cols_hbm.at[:, at], cols.at[:, at], strip_sems.at[2 * q]),
            pltpu.make_async_copy(summed_hbm.at[:, at], summed.at[:, at], strip_sems.at[2 * q + 1]),
        ]

    for q in range(4):
        for load in strip_loads(q):
            load.start()
    for load in loads:
        load.wait()

    for n in range(4):
        at = slice(n * 256, n * 256 + 256)
        inv_hi[at, :], inv_lo[at, :] = split2(inverse[at, :])

    @pl.loop(0, 4)
    def _(m):
        at = pl.ds(pl.multiple_of(m * 256, 256), 256)
        left = split2(rows[at, :])
        for n in range(4):
            past = slice(0, n * 256 + 256)
            here = slice(n * 256, n * 256 + 256)
            solved[at, here] = product(
                [part[:, past] for part in left], (inv_hi[here, past], inv_lo[here, past]), ((1,), (1,))
            )

    @pl.when(my_row < 2)
    def _():
        load = pltpu.make_async_copy(lower_hbm, solved.at[pl.ds(0, NB)], in_sems.at[2])
        load.start()
        load.wait()

    stores = [
        pltpu.make_async_copy(solved.at[pl.ds(b * NB, NB)], factor_hbm.at[b], factor_sems.at[b])
        for b in range(2)
    ]
    for store in stores:
        store.start()
    for n in range(4):
        at = slice(n * 256, n * 256 + 256)
        sol_hi[at, :], sol_lo[at, :] = split2(solved[at, :])

    for q in range(4):
        strip = slice(q * NB, q * NB + NB)
        for load in strip_loads(q):
            load.wait()
        for n in range(4):
            at = slice(n * 256, n * 256 + 256)
            col_hi[at, :], col_lo[at, :] = split2(cols[at, strip])
        for n in range(4):
            past = slice(0, n * 256 + 256)
            here = slice(n * 256, n * 256 + 256)
            value = product(
                (inv_hi[here, past], inv_lo[here, past]), (col_hi[past, :], col_lo[past, :]), ((1,), (0,))
            )
            y_hi[here, :], y_lo[here, :] = split2(value)

        @pl.loop(0, 4)
        def _(m):
            at = pl.ds(pl.multiple_of(m * 256, 256), 256)
            summed[at, strip] -= product(
                (sol_hi[at, :], sol_lo[at, :]), (y_hi[...], y_lo[...]), ((1,), (0,))
            )

        for b in range(2):
            store = pltpu.make_async_copy(
                summed.at[pl.ds(b * NB, NB), pl.ds(q * NB, NB)], schur_hbm.at[b, :, q, :], out_sems.at[2 * q + b]
            )
            store.start()
            stores.append(store)
    for store in stores:
        store.wait()


def update(summed, rows, cols, lower, inverse):
    anyspace = pl.BlockSpec(memory_space=pl.ANY)
    return pl.pallas_call(
        update_kernel,
        out_shape=(
            jax.ShapeDtypeStruct((2, NB, 4, NB), F32),
            jax.ShapeDtypeStruct((2, NB, 2 * NB), F32),
        ),
        in_specs=[anyspace] * 5,
        out_specs=[anyspace] * 2,
        scratch_shapes=[
            VM((1024, 2048), F32),
            VM((1024, 1024), F32),
            VM((1024, 2048), F32),
            VM((1024, 1024), F32),
            VM((1024, 1024), F32),
            VM((1024, 1024), BF),
            VM((1024, 1024), BF),
            VM((1024, 1024), BF),
            VM((1024, 1024), BF),
            VM((1024, NB), BF),
            VM((1024, NB), BF),
            VM((1024, NB), BF),
            VM((1024, NB), BF),
            pltpu.SemaphoreType.DMA((3,)),
            pltpu.SemaphoreType.DMA((8,)),
            pltpu.SemaphoreType.DMA((8,)),
            pltpu.SemaphoreType.DMA((2,)),
        ],
        compiler_params=pltpu.CompilerParams(vmem_limit_bytes=60 << 20),
    )(summed, rows, cols, lower, inverse)


def on_device(front, child_blocks, index_maps):
    summed = exchange(front, child_blocks, index_maps, lax.axis_size("row"), lax.axis_size("col"))
    rows, cols, lower, inverse = share(summed)
    return update(summed, rows, cols, lower, inverse)


def solution(mesh):
    placed = (P(None, "row", None, "col"), P(None, "row", "col"), P())
    return jax.shard_map(
        on_device,
        mesh=mesh,
        in_specs=placed,
        out_specs=(P(None, "row", None, "col"), P(None, "row", None)),
        check_vma=False,
    )
```

```python
import functools

import jax
import jax.numpy as jnp
from jax import lax
from jax.experimental import pallas as pl
from jax.experimental.pallas import tpu as pltpu
from jax.sharding import PartitionSpec as P

NB = 512
MESH = pl.DeviceIdType.MESH
BF = jnp.bfloat16
F32 = jnp.float32
VM = pltpu.VMEM
HI = lax.Precision.HIGHEST


def split2(value):
    first = value.astype(BF)
    return first, (value - first.astype(F32)).astype(BF)


def dot(left, right):
    return jnp.dot(left, right, preferred_element_type=F32)


def dot_nn(a,b): return lax.dot_general(a,b,(((1,),(0,)),((),())),precision=HI,preferred_element_type=F32)
def dot_nt(a,b): return lax.dot_general(a,b,(((1,),(1,)),((),())),precision=HI,preferred_element_type=F32)

def inverse_factor(block):
    n, group = 128, 8
    full = (8, n)
    lane = lax.broadcasted_iota(jnp.int32, full, 1)
    sub = lax.broadcasted_iota(jnp.int32, full, 0)
    tiles = [block[8 * i:8 * i + 8, :] for i in range(n // 8)]
    for at in range(n // 8):
        j = at * group
        inside = (lane >= j) & (lane < j + group)
        first = [jnp.broadcast_to(tiles[at][:, j + a:j + a + 1], full) for a in range(group)]
        pivots = [
            [jnp.broadcast_to(first[a][b:b + 1, :], full) for a in range(b + 1)] for b in range(group)
        ]
        solved = []
        for a in range(group):
            row = jnp.broadcast_to(tiles[at][a:a + 1, :], full)
            solved.append(jnp.where(lane == j + a, 1.0, jnp.where(inside, 0.0, row)))
        factors = [[None] * group for _ in range(group)]
        inverses = [None] * group
        for a in range(group):
            inverses[a] = 1.0 / pivots[a][a]
            for b in range(a + 1, group):
                factors[b][a] = pivots[b][a] * inverses[a]
            for b in range(a + 1, group):
                for c in range(a + 1, b + 1):
                    pivots[b][c] = pivots[b][c] - factors[b][a] * pivots[c][a]
                solved[b] = solved[b] - factors[b][a] * solved[a]
        lines = [inverses[b] * solved[b] for b in range(group)]
        for a in range(group - 2, -1, -1):
            for b in range(a + 1, group):
                lines[a] = lines[a] - factors[b][a] * lines[b]
        made = tiles[at]
        for b in range(group):
            made = jnp.where(sub == b, jnp.where(lane == j + b, pivots[b][b], solved[b]), made)
        tiles[at] = made
        for i in range(at + 1, n // 8):
            value = jnp.where(inside, 0.0, tiles[i])
            for a in range(group):
                value = value - jnp.broadcast_to(tiles[i][:, j + a:j + a + 1], full) * lines[a]
            tiles[i] = value
    whole = jnp.concatenate(tiles, axis=0)
    r = lax.broadcasted_iota(jnp.int32, (n, n), 0)
    c = lax.broadcasted_iota(jnp.int32, (n, n), 1)
    diag = jnp.sum(jnp.where(r == c, whole, 0.0), axis=1, keepdims=True)
    unit = jnp.where(r > c, whole, jnp.where(r == c, 1.0, 0.0))
    return unit * (1.0 / jnp.sqrt(diag))


def factor_leading(lead, lower, inverse, work, corner, between):
    n = 128
    r = lax.broadcasted_iota(jnp.int32, (n, n), 0)
    c = lax.broadcasted_iota(jnp.int32, (n, n), 1)
    work[...] = lead[...]
    lower[...] = jnp.zeros_like(lower)
    inverse[...] = jnp.zeros_like(inverse)

    @pl.loop(0, 8)
    def _(j):
        at = pl.ds(pl.multiple_of(j * n, n), n)
        corner[...] = inverse_factor(work[at, at])
        for s in range(8):
            @pl.when(j == s)
            def _():
                at = slice(s * n, s * n + n)
                w = corner[...]
                lower[at, at] = jnp.where(r >= c, dot_nt(work[at, at], w), 0.0)
                inverse[at, at] = w
                if s < 7:
                    p = dot_nt(work[s * n + n:, at], w)
                    lower[s * n + n:, at] = p
                    for k in range(s + 1, 8):
                        o = (k - s - 1) * n
                        work[k * n:, k * n:k * n + n] -= dot_nt(p[o:], p[o:o + n])
                if s:
                    done = slice(0, s * n)
                    inverse[at, done] = -dot_nn(w, dot_nn(lower[at, done], inverse[done, done]))
                if s in between:
                    between[s]()


def front_kernel(rows, cols, child_ref, front_ref, row_ids_ref, col_ids_ref,
                 summed_out, rows_out, cols_out, lower_out, inverse_out,
                 staged, grouped, received, summed, stacked, row_maps, rows_ref, cols_ref, lead_ref,
                 lower, inverse, corner, child_sem, front_sems, send_sems, recv_sem, sent, got, out_sems):
    my_row = lax.axis_index("row")
    my_col = lax.axis_index("col")
    y, z = my_row // 4, my_row % 4
    x, core = my_col // 2, my_col % 2
    chip = my_row * 4 + x
    wait_bytes = cols_ref
    for h in range(2):
        pltpu.make_async_copy(child_ref.at[h], staged.at[pl.ds(h * NB, NB)], child_sem).start()
    for b in range(2):
        for q in range(4):
            pltpu.make_async_copy(
                front_ref.at[b, :, q, :],
                summed.at[pl.ds(b * NB, NB), pl.ds(q * NB, NB)],
                front_sems.at[b * 4 + q],
            ).start()
    pltpu.make_async_copy(staged, staged, child_sem).wait()

    def group_rows(k):
        lanes = lax.broadcasted_iota(jnp.int32, (32, 128), 1) // 32
        at = pl.ds(pl.multiple_of(k * 32, 32), 32)
        for h in range(2):
            source_at = pl.ds(pl.multiple_of(h * NB + k * 32, 32), 32)
            tiles = [staged[source_at, t * 128:(t + 1) * 128] for t in range(8)]
            for dest in range(8):
                made = None
                for part in range(4):
                    source = tiles[part * 2 + dest // 4]
                    shift = (part * 32 - (dest % 4) * 32) % 128
                    moved = pltpu.roll(source, shift, axis=1) if shift else source
                    made = moved if made is None else jnp.where(lanes == part, moved, made)
                grouped[h, at, dest * 128:(dest + 1) * 128] = made

    def block(ref, row, col):
        return ref.at[
            :, pl.ds(pl.multiple_of(row * 32, 32), 32), pl.ds(pl.multiple_of(col * 128, 128), 128)
        ]

    def send(k, dest, sem):
        pltpu.make_async_remote_copy(
            src_ref=block(grouped, k, dest),
            dst_ref=block(received, my_row, my_col),
            send_sem=send_sems.at[sem],
            recv_sem=recv_sem,
            device_id=(k, dest),
            device_id_type=MESH,
        ).start()

    @pl.loop(0, rows)
    def _(t):
        k = lax.rem(my_row + t, rows)
        group_rows(k)
        for u in range(1, cols):
            send(k, lax.rem(my_col + u, cols), 0)

        @pl.when(t > 0)
        def _():
            send(k, my_col, 1)

    own = pltpu.make_async_copy(
        block(grouped, my_row, my_col), block(received, my_row, my_col), recv_sem
    )
    own.start()
    for b in range(2):
        for q in range(4):
            pltpu.make_async_copy(
                front_ref.at[b, :, q, :],
                summed.at[pl.ds(b * NB, NB), pl.ds(q * NB, NB)],
                front_sems.at[b * 4 + q],
            ).wait()
    for h in range(2):
        chosen = (
            lax.broadcasted_iota(jnp.int32, (1024, 512), 0) == row_ids_ref[h:h + 1, :]
        ).astype(BF)
        row_maps[h, :, 0:512] = chosen
        row_maps[h, :, 512:1024] = chosen
    pltpu.make_async_copy(received, received, recv_sem).wait()
    for h in range(2):
        for r in (0, 256):
            stacked[h, r:r + 256, :], stacked[h, 512 + r:768 + r, :] = split2(received[h, r:r + 256, :])

    def add_children(n):
        at = pl.ds(pl.multiple_of(n * 256, 256), 256)
        total = summed[:, at]
        for h in range(2):
            col_map = (
                lax.broadcasted_iota(jnp.int32, (1024, 256), 1) + n * 256 == col_ids_ref[h]
            ).astype(BF)
            total += dot(row_maps[h], dot(stacked[h], col_map).astype(BF))
        summed[:, at] = total

    early = jnp.where(my_col < 2, 2, 0)

    @pl.loop(0, early)
    def _(n):
        add_children(n)

    def remote(src, dst, phase, row, col, send_phase=None):
        leaving = sent.at[phase if send_phase is None else send_phase]
        pltpu.make_async_remote_copy(
            src_ref=src, dst_ref=dst, send_sem=leaving, recv_sem=got.at[phase],
            device_id=(row, col), device_id_type=MESH,
        ).start()

    def local(src, dst, phase):
        pltpu.make_async_copy(src, dst, got.at[phase]).start()

    def wait(sem, ref):
        pltpu.make_async_copy(ref, ref, sem).wait()

    def rows_of(ref, start, size, cols=None):
        at = pl.ds(pl.multiple_of(start, 8), size)
        if cols is None:
            return ref.at[at]
        return ref.at[at, pl.ds(cols[0], cols[1])]

    def lead_piece(ref, block, m):
        if block == 0:
            return rows_of(ref, m * 8, 8, (0, 512))
        if block == 1:
            return rows_of(ref, 512 + m * 8, 8, (0, 256))
        if block == 2:
            return rows_of(ref, 512 + m * 8, 8, (256, 256))
        return rows_of(ref, 512 + m * 8, 8, (512, 512))

    def summed_piece(block, m):
        if block == 1:
            return rows_of(summed, m * 8, 8, (0, 256))
        if block == 2:
            return rows_of(summed, m * 8, 8, (256, 256))
        return rows_of(summed, m * 8, 8, (0, 512))

    for owner_row, owner_col, blocks in ((0, 0, (0,)), (1, 0, (1, 2)), (1, 1, (3,))):
        @pl.when((my_row == owner_row) & (my_col == owner_col))
        def _():
            for block in blocks:
                target_core = 0 if block < 2 else 1

                @pl.loop(0, 64)
                def _(m):
                    row, col = m // 4, (m % 4) * 2 + target_core
                    here = (row == owner_row) & (col == owner_col)

                    @pl.when(here)
                    def _():
                        local(summed_piece(block, m), lead_piece(lead_ref, block, m), 0)

                    @pl.when(jnp.logical_not(here))
                    def _():
                        remote(
                            summed_piece(block, m), lead_piece(lead_ref, block, m), 0, row, col,
                            11 if block == 2 else 0,
                        )

    for src in range(2):
        @pl.when(my_col == src)
        def _():
            for k in range(4):
                piece = rows_of(summed, k * 256, 256, (0, 512))
                place = rows_of(rows_ref, k * 256, 256, (src * 512, 512))
                if k == 0:
                    local(piece, place, 2)
                else:
                    remote(piece, place, 2, my_row, 2 * k + src)

    @pl.loop(early, 4)
    def _(n):
        add_children(n)

    @pl.when(core == 0)
    def _():
        wait(got.at[0], wait_bytes.at[pl.ds(0, 8), pl.ds(0, 768)])

        @pl.loop(1, 64)
        def _(t):
            other = lax.rem(chip + t, 64)
            for block in (0, 1):
                remote(lead_piece(lead_ref, block, chip), lead_piece(lead_ref, block, chip), 3, other // 4, (other % 4) * 2)

    @pl.when(core == 1)
    def _():
        wait(got.at[0], wait_bytes.at[pl.ds(0, 8), pl.ds(0, 768)])

        @pl.loop(1, 64)
        def _(t):
            other = lax.rem(chip + t, 64)
            for block in (2, 3):
                remote(lead_piece(lead_ref, block, chip), lead_piece(lead_ref, block, chip), 3, other // 4, (other % 4) * 2 + 1)

    wait(got.at[2], rows_of(wait_bytes, 0, 256, (0, 512)))
    for core_is in range(2):
        @pl.when(core == core_is)
        def _():
            for t in range(1, 4):
                piece = rows_of(rows_ref, x * 256, 256, (core_is * 512, 512))
                remote(piece, piece, 4, my_row, lax.rem(x + t, 4) * 2 + core_is)

    @pl.loop(4, 8)
    def _(n):
        add_children(n)

    for src in range(2):
        @pl.when(my_row == src)
        def _():
            for k in range(16):
                piece = rows_of(summed, k * 32, 32)
                place = rows_of(cols_ref, src * NB + k * 32, 32)
                if k == src:
                    local(piece, place, 1)
                else:
                    remote(piece, place, 1, k, my_col)

    pltpu.make_async_copy(summed, summed_out, out_sems.at[4]).start()

    wait(got.at[3], rows_of(wait_bytes, 0, 504, (0, 768)))
    for core_is in range(2):
        @pl.when(core == core_is)
        def _():
            if core_is == 0:
                pieces = [lead_ref.at[pl.ds(0, 512), pl.ds(0, 512)], lead_ref.at[pl.ds(512, 512), pl.ds(0, 256)]]
            else:
                pieces = [lead_ref.at[pl.ds(512, 512), pl.ds(256, 256)], lead_ref.at[pl.ds(512, 512), pl.ds(512, 512)]]
            for piece in pieces:
                remote(piece, piece, 7, my_row, x * 2 + 1 - core_is)

    def first_step():
        wait(got.at[1], rows_of(wait_bytes, 0, 64, (0, 2048)))
        for src in range(2):
            left = rows_of(cols_ref, src * NB + my_row * 32, 32, (0, 1024))
            right = rows_of(cols_ref, src * NB + my_row * 32, 32, (1024, 1024))
            for t in range(1, 4):
                remote(left, left, 5, y * 4 + lax.rem(z + t, 4), my_col)
                remote(right, right, 6, lax.rem(y + t, 4) * 4 + z, my_col)

    def second_step():
        wait(got.at[5], rows_of(wait_bytes, 0, 192, (0, 1024)))
        wait(got.at[6], rows_of(wait_bytes, 0, 192, (0, 1024)))
        for src in range(2):
            left = rows_of(cols_ref, src * NB + y * 128, 128, (0, 1024))
            for t in range(1, 4):
                remote(left, left, 8, lax.rem(y + t, 4) * 4 + z, my_col)
            for k in range(4):
                right = rows_of(cols_ref, src * NB + k * 128 + z * 32, 32, (1024, 1024))
                for t in range(1, 4):
                    remote(right, right, 9, y * 4 + lax.rem(z + t, 4), my_col)

    def other_core():
        wait(got.at[4], rows_of(wait_bytes, 0, 768, (0, 512)))
        for core_is in range(2):
            @pl.when(core == core_is)
            def _():
                piece = rows_ref.at[:, pl.ds(core_is * 512, 512)]
                remote(piece, piece, 10, my_row, x * 2 + 1 - core_is)

    wait(got.at[7], rows_of(wait_bytes, 0, 512, (0, 768)))
    factor_leading(lead_ref, lower, inverse, staged, corner, {0: first_step, 2: second_step, 4: other_core})
    outs = [
        pltpu.make_async_copy(inverse, inverse_out, out_sems.at[0]),
        pltpu.make_async_copy(rows_ref, rows_out, out_sems.at[1]),
        pltpu.make_async_copy(cols_ref, cols_out, out_sems.at[2]),
    ]
    outs[0].start()
    for src in range(2):
        @pl.when(my_row == src)
        def _():
            pltpu.make_async_copy(lower.at[pl.ds(src * NB, NB)], lower_out, out_sems.at[3]).start()
    wait(got.at[8], rows_of(wait_bytes, 0, 768, (0, 1024)))
    wait(got.at[9], rows_of(wait_bytes, 0, 768, (0, 1024)))
    wait(got.at[10], rows_of(wait_bytes, 0, 1024, (0, 512)))

    outs[1].start()
    outs[2].start()

    @pl.when((my_row == 0) & (my_col == 0))
    def _():
        wait(sent.at[0], rows_of(wait_bytes, 0, 504, (0, 512)))

    @pl.when((my_row == 1) & (my_col == 0))
    def _():
        wait(sent.at[0], rows_of(wait_bytes, 0, 504, (0, 256)))
        wait(sent.at[11], rows_of(wait_bytes, 0, 512, (0, 256)))

    @pl.when((my_row == 1) & (my_col == 1))
    def _():
        wait(sent.at[0], rows_of(wait_bytes, 0, 504, (0, 512)))

    @pl.when(my_row < 2)
    def _():
        wait(sent.at[1], rows_of(wait_bytes, 0, 480, (0, 2048)))

    @pl.when(my_col < 2)
    def _():
        wait(sent.at[2], rows_of(wait_bytes, 0, 768, (0, 512)))

    wait(sent.at[3], rows_of(wait_bytes, 0, 504, (0, 768)))
    wait(sent.at[4], rows_of(wait_bytes, 0, 768, (0, 512)))
    wait(sent.at[5], rows_of(wait_bytes, 0, 192, (0, 1024)))
    wait(sent.at[6], rows_of(wait_bytes, 0, 192, (0, 1024)))
    wait(sent.at[7], rows_of(wait_bytes, 0, 512, (0, 768)))
    wait(sent.at[8], rows_of(wait_bytes, 0, 768, (0, 1024)))
    wait(sent.at[9], rows_of(wait_bytes, 0, 768, (0, 1024)))
    wait(sent.at[10], rows_of(wait_bytes, 0, 1024, (0, 512)))
    for out in outs:
        out.wait()

    @pl.when(my_row < 2)
    def _():
        pltpu.make_async_copy(lower.at[pl.ds(0, NB)], lower_out, out_sems.at[3]).wait()

    pltpu.make_async_copy(
        grouped.at[:, :, pl.ds(0, 896)], grouped.at[:, :, pl.ds(0, 896)], send_sems.at[0]
    ).wait()
    pltpu.make_async_copy(
        grouped.at[:, pl.ds(0, 480), pl.ds(0, 128)],
        grouped.at[:, pl.ds(0, 480), pl.ds(0, 128)],
        send_sems.at[1],
    ).wait()
    pltpu.make_async_copy(summed, summed_out, out_sems.at[4]).wait()


def local_position(ids, count):
    return ids // (NB * count) * NB + ids % NB


def id_tables(index_maps, rows, cols):
    my_row = lax.axis_index("row")
    my_col = lax.axis_index("col")
    ratio = rows // cols
    row_ids = lax.dynamic_index_in_dim(
        index_maps.reshape(2, rows, rows, -1), my_row, 2, keepdims=False
    ).reshape(2, -1)
    col_ids = lax.dynamic_index_in_dim(
        index_maps.reshape(2, cols, ratio, ratio, cols, -1), my_col, 4, keepdims=False
    ).reshape(2, -1)
    return local_position(row_ids, rows), local_position(col_ids, cols)[:, :, None]


def assemble(front, child_blocks, index_maps, rows, cols):
    row_ids, col_ids = id_tables(index_maps, rows, cols)
    vm = pl.BlockSpec(memory_space=pltpu.VMEM)
    anyspace = pl.BlockSpec(memory_space=pl.ANY)
    dma = pltpu.SemaphoreType.DMA
    return pl.pallas_call(
        functools.partial(front_kernel, rows, cols),
        out_shape=(
            jax.ShapeDtypeStruct((1024, 2048), F32),
            jax.ShapeDtypeStruct((1024, 1024), F32),
            jax.ShapeDtypeStruct((1024, 2048), F32),
            jax.ShapeDtypeStruct((512, 1024), F32),
            jax.ShapeDtypeStruct((1024, 1024), F32),
        ),
        in_specs=[anyspace, anyspace, vm, vm],
        out_specs=[anyspace] * 5,
        scratch_shapes=[
            VM((1024, 1024), F32),
            VM((2, 512, 1024), F32),
            VM((2, 512, 1024), F32),
            VM((1024, 2048), F32),
            VM((2, 1024, 1024), BF),
            VM((2, 1024, 1024), BF),
            VM((1024, 1024), F32),
            VM((1024, 2048), F32),
            VM((1024, 1024), F32),
            VM((1024, 1024), F32),
            VM((1024, 1024), F32),
            VM((128, 128), F32),
            dma,
            dma((8,)),
            dma((2,)),
            dma,
            dma((12,)),
            dma((12,)),
            dma((5,)),
        ],
        compiler_params=pltpu.CompilerParams(vmem_limit_bytes=62 << 20, has_side_effects=True),
    )(child_blocks, front, row_ids, col_ids)


def product(left, right, dims):
    parts = [(0, 0), (0, 1), (1, 0)]
    total = None
    for a, b in parts:
        term = lax.dot_general(left[a], right[b], (dims, ((), ())), preferred_element_type=F32)
        total = term if total is None else total + term
    return total


def update_kernel(summed_hbm, rows_hbm, cols_hbm, lower_hbm, inverse_hbm, schur_hbm, factor_hbm,
                  summed, rows, cols, inverse, solved, inv_hi, inv_lo, sol_hi, sol_lo,
                  col_hi, col_lo, y_hi, y_lo, in_sems, strip_sems, out_sems, factor_sems):
    my_row = lax.axis_index("row")
    loads = [
        pltpu.make_async_copy(inverse_hbm, inverse, in_sems.at[0]),
        pltpu.make_async_copy(rows_hbm, rows, in_sems.at[1]),
    ]
    for load in loads:
        load.start()

    def strip_loads(q):
        at = pl.ds(q * NB, NB)
        return [
            pltpu.make_async_copy(cols_hbm.at[:, at], cols.at[:, at], strip_sems.at[2 * q]),
            pltpu.make_async_copy(summed_hbm.at[:, at], summed.at[:, at], strip_sems.at[2 * q + 1]),
        ]

    for q in range(4):
        for load in strip_loads(q):
            load.start()
    for load in loads:
        load.wait()

    for n in range(4):
        at = slice(n * 256, n * 256 + 256)
        inv_hi[at, :], inv_lo[at, :] = split2(inverse[at, :])

    @pl.loop(0, 4)
    def _(m):
        at = pl.ds(pl.multiple_of(m * 256, 256), 256)
        left = split2(rows[at, :])
        for n in range(4):
            past = slice(0, n * 256 + 256)
            here = slice(n * 256, n * 256 + 256)
            solved[at, here] = product(
                [part[:, past] for part in left], (inv_hi[here, past], inv_lo[here, past]), ((1,), (1,))
            )

    @pl.when(my_row < 2)
    def _():
        load = pltpu.make_async_copy(lower_hbm, solved.at[pl.ds(0, NB)], in_sems.at[2])
        load.start()
        load.wait()

    stores = [
        pltpu.make_async_copy(solved.at[pl.ds(b * NB, NB)], factor_hbm.at[b], factor_sems.at[b])
        for b in range(2)
    ]
    for store in stores:
        store.start()
    for n in range(4):
        at = slice(n * 256, n * 256 + 256)
        sol_hi[at, :], sol_lo[at, :] = split2(solved[at, :])

    for q in range(4):
        strip = slice(q * NB, q * NB + NB)
        for load in strip_loads(q):
            load.wait()
        for n in range(4):
            at = slice(n * 256, n * 256 + 256)
            col_hi[at, :], col_lo[at, :] = split2(cols[at, strip])
        for n in range(4):
            past = slice(0, n * 256 + 256)
            here = slice(n * 256, n * 256 + 256)
            value = product(
                (inv_hi[here, past], inv_lo[here, past]), (col_hi[past, :], col_lo[past, :]), ((1,), (0,))
            )
            y_hi[here, :], y_lo[here, :] = split2(value)

        @pl.loop(0, 4)
        def _(m):
            at = pl.ds(pl.multiple_of(m * 256, 256), 256)
            summed[at, strip] -= product(
                (sol_hi[at, :], sol_lo[at, :]), (y_hi[...], y_lo[...]), ((1,), (0,))
            )

        for b in range(2):
            store = pltpu.make_async_copy(
                summed.at[pl.ds(b * NB, NB), pl.ds(q * NB, NB)], schur_hbm.at[b, :, q, :], out_sems.at[2 * q + b]
            )
            store.start()
            stores.append(store)
    for store in stores:
        store.wait()


def update(summed, rows, cols, lower, inverse):
    anyspace = pl.BlockSpec(memory_space=pl.ANY)
    return pl.pallas_call(
        update_kernel,
        out_shape=(
            jax.ShapeDtypeStruct((2, NB, 4, NB), F32),
            jax.ShapeDtypeStruct((2, NB, 2 * NB), F32),
        ),
        in_specs=[anyspace] * 5,
        out_specs=[anyspace] * 2,
        scratch_shapes=[
            VM((1024, 2048), F32),
            VM((1024, 1024), F32),
            VM((1024, 2048), F32),
            VM((1024, 1024), F32),
            VM((1024, 1024), F32),
            VM((1024, 1024), BF),
            VM((1024, 1024), BF),
            VM((1024, 1024), BF),
            VM((1024, 1024), BF),
            VM((1024, NB), BF),
            VM((1024, NB), BF),
            VM((1024, NB), BF),
            VM((1024, NB), BF),
            pltpu.SemaphoreType.DMA((3,)),
            pltpu.SemaphoreType.DMA((8,)),
            pltpu.SemaphoreType.DMA((8,)),
            pltpu.SemaphoreType.DMA((2,)),
        ],
        compiler_params=pltpu.CompilerParams(vmem_limit_bytes=60 << 20),
    )(summed, rows, cols, lower, inverse)


def on_device(front, child_blocks, index_maps):
    parts = assemble(front, child_blocks, index_maps, lax.axis_size("row"), lax.axis_size("col"))
    return update(*parts)


def solution(mesh):
    placed = (P(None, "row", None, "col"), P(None, "row", "col"), P())
    return jax.shard_map(
        on_device,
        mesh=mesh,
        in_specs=placed,
        out_specs=(P(None, "row", None, "col"), P(None, "row", None)),
        check_vma=False,
    )
```

```python
import functools

import jax
import jax.numpy as jnp
from jax import lax
from jax.experimental import pallas as pl
from jax.experimental.pallas import tpu as pltpu
from jax.sharding import PartitionSpec as P

NB = 512
MESH = pl.DeviceIdType.MESH
BF = jnp.bfloat16
F32 = jnp.float32
VM = pltpu.VMEM
HI = lax.Precision.HIGHEST


def split2(value):
    first = value.astype(BF)
    return first, (value - first.astype(F32)).astype(BF)


def product(left, right, dims):
    parts = [(0, 0), (0, 1), (1, 0)]
    total = None
    for a, b in parts:
        term = lax.dot_general(left[a], right[b], (dims, ((), ())), preferred_element_type=F32)
        total = term if total is None else total + term
    return total


def dot(left, right):
    return jnp.dot(left, right, preferred_element_type=F32)


def dot_nn(a,b): return lax.dot_general(a,b,(((1,),(0,)),((),())),precision=HI,preferred_element_type=F32)
def dot_nt(a,b): return lax.dot_general(a,b,(((1,),(1,)),((),())),precision=HI,preferred_element_type=F32)

def inverse_factor(block):
    n, group = 128, 8
    full = (8, n)
    lane = lax.broadcasted_iota(jnp.int32, full, 1)
    sub = lax.broadcasted_iota(jnp.int32, full, 0)
    tiles = [block[8 * i:8 * i + 8, :] for i in range(n // 8)]
    for at in range(n // 8):
        j = at * group
        inside = (lane >= j) & (lane < j + group)
        first = [jnp.broadcast_to(tiles[at][:, j + a:j + a + 1], full) for a in range(group)]
        pivots = [
            [jnp.broadcast_to(first[a][b:b + 1, :], full) for a in range(b + 1)] for b in range(group)
        ]
        solved = []
        for a in range(group):
            row = jnp.broadcast_to(tiles[at][a:a + 1, :], full)
            solved.append(jnp.where(lane == j + a, 1.0, jnp.where(inside, 0.0, row)))
        factors = [[None] * group for _ in range(group)]
        inverses = [None] * group
        for a in range(group):
            inverses[a] = 1.0 / pivots[a][a]
            for b in range(a + 1, group):
                factors[b][a] = pivots[b][a] * inverses[a]
            for b in range(a + 1, group):
                for c in range(a + 1, b + 1):
                    pivots[b][c] = pivots[b][c] - factors[b][a] * pivots[c][a]
                solved[b] = solved[b] - factors[b][a] * solved[a]
        lines = [inverses[b] * solved[b] for b in range(group)]
        for a in range(group - 2, -1, -1):
            for b in range(a + 1, group):
                lines[a] = lines[a] - factors[b][a] * lines[b]
        made = tiles[at]
        for b in range(group):
            made = jnp.where(sub == b, jnp.where(lane == j + b, pivots[b][b], solved[b]), made)
        tiles[at] = made
        for i in range(at + 1, n // 8):
            value = jnp.where(inside, 0.0, tiles[i])
            for a in range(group):
                value = value - jnp.broadcast_to(tiles[i][:, j + a:j + a + 1], full) * lines[a]
            tiles[i] = value
    whole = jnp.concatenate(tiles, axis=0)
    r = lax.broadcasted_iota(jnp.int32, (n, n), 0)
    c = lax.broadcasted_iota(jnp.int32, (n, n), 1)
    diag = jnp.sum(jnp.where(r == c, whole, 0.0), axis=1, keepdims=True)
    unit = jnp.where(r > c, whole, jnp.where(r == c, 1.0, 0.0))
    return unit * (1.0 / jnp.sqrt(diag))


def factor_leading(lead, lower, inverse, work, corner, between):
    n = 128
    r = lax.broadcasted_iota(jnp.int32, (n, n), 0)
    c = lax.broadcasted_iota(jnp.int32, (n, n), 1)
    work[...] = lead[...]
    lower[...] = jnp.zeros_like(lower)
    inverse[...] = jnp.zeros_like(inverse)

    @pl.loop(0, 8)
    def _(j):
        at = pl.ds(pl.multiple_of(j * n, n), n)
        corner[...] = inverse_factor(work[at, at])
        for s in range(8):
            @pl.when(j == s)
            def _():
                at = slice(s * n, s * n + n)
                w = corner[...]
                lower[at, at] = jnp.where(r >= c, dot_nt(work[at, at], w), 0.0)
                inverse[at, at] = w
                if s < 7:
                    p = dot_nt(work[s * n + n:, at], w)
                    lower[s * n + n:, at] = p
                    for k in range(s + 1, 8):
                        o = (k - s - 1) * n
                        work[k * n:, k * n:k * n + n] -= dot_nt(p[o:], p[o:o + n])
                if s:
                    done = slice(0, s * n)
                    inverse[at, done] = -dot_nn(w, dot_nn(lower[at, done], inverse[done, done]))
                if s in between:
                    between[s]()


def front_kernel(rows, cols, child_ref, front_ref, row_ids_ref, col_ids_ref,
                 summed_out, factor_out, inverse_out, right_out, left_out,
                 staged, grouped, received, summed, stacked, row_maps, rows_ref, cols_ref, lead_ref,
                 lower, inverse, corner, col_hi, col_lo, child_sem, front_sems, send_sems, recv_sem, sent, got, out_sems):
    my_row = lax.axis_index("row")
    my_col = lax.axis_index("col")
    y, z = my_row // 4, my_row % 4
    x, core = my_col // 2, my_col % 2
    chip = my_row * 4 + x
    wait_bytes = cols_ref
    for h in range(2):
        pltpu.make_async_copy(child_ref.at[h], staged.at[pl.ds(h * NB, NB)], child_sem).start()
    for b in range(2):
        for q in range(4):
            pltpu.make_async_copy(
                front_ref.at[b, :, q, :],
                summed.at[pl.ds(b * NB, NB), pl.ds(q * NB, NB)],
                front_sems.at[b * 4 + q],
            ).start()
    pltpu.make_async_copy(staged, staged, child_sem).wait()

    def group_rows(k):
        lanes = lax.broadcasted_iota(jnp.int32, (32, 128), 1) // 32
        at = pl.ds(pl.multiple_of(k * 32, 32), 32)
        for h in range(2):
            source_at = pl.ds(pl.multiple_of(h * NB + k * 32, 32), 32)
            tiles = [staged[source_at, t * 128:(t + 1) * 128] for t in range(8)]
            for dest in range(8):
                made = None
                for part in range(4):
                    source = tiles[part * 2 + dest // 4]
                    shift = (part * 32 - (dest % 4) * 32) % 128
                    moved = pltpu.roll(source, shift, axis=1) if shift else source
                    made = moved if made is None else jnp.where(lanes == part, moved, made)
                grouped[h, at, dest * 128:(dest + 1) * 128] = made

    def block(ref, row, col):
        return ref.at[
            :, pl.ds(pl.multiple_of(row * 32, 32), 32), pl.ds(pl.multiple_of(col * 128, 128), 128)
        ]

    def send(k, dest, sem):
        pltpu.make_async_remote_copy(
            src_ref=block(grouped, k, dest),
            dst_ref=block(received, my_row, my_col),
            send_sem=send_sems.at[sem],
            recv_sem=recv_sem,
            device_id=(k, dest),
            device_id_type=MESH,
        ).start()

    @pl.loop(0, rows)
    def _(t):
        k = lax.rem(my_row + t, rows)
        group_rows(k)
        for u in range(1, cols):
            send(k, lax.rem(my_col + u, cols), 0)

        @pl.when(t > 0)
        def _():
            send(k, my_col, 1)

    own = pltpu.make_async_copy(
        block(grouped, my_row, my_col), block(received, my_row, my_col), recv_sem
    )
    own.start()
    for b in range(2):
        for q in range(4):
            pltpu.make_async_copy(
                front_ref.at[b, :, q, :],
                summed.at[pl.ds(b * NB, NB), pl.ds(q * NB, NB)],
                front_sems.at[b * 4 + q],
            ).wait()
    for h in range(2):
        chosen = (
            lax.broadcasted_iota(jnp.int32, (1024, 512), 0) == row_ids_ref[h:h + 1, :]
        ).astype(BF)
        row_maps[h, :, 0:512] = chosen
        row_maps[h, :, 512:1024] = chosen
    pltpu.make_async_copy(received, received, recv_sem).wait()
    for h in range(2):
        for r in (0, 256):
            stacked[h, r:r + 256, :], stacked[h, 512 + r:768 + r, :] = split2(received[h, r:r + 256, :])

    def add_children(n):
        at = pl.ds(pl.multiple_of(n * 256, 256), 256)
        total = summed[:, at]
        for h in range(2):
            col_map = (
                lax.broadcasted_iota(jnp.int32, (1024, 256), 1) + n * 256 == col_ids_ref[h]
            ).astype(BF)
            total += dot(row_maps[h], dot(stacked[h], col_map).astype(BF))
        summed[:, at] = total

    early = jnp.where(my_col < 2, 2, 0)

    @pl.loop(0, early)
    def _(n):
        add_children(n)

    def remote(src, dst, phase, row, col, send_phase=None):
        leaving = sent.at[phase if send_phase is None else send_phase]
        pltpu.make_async_remote_copy(
            src_ref=src, dst_ref=dst, send_sem=leaving, recv_sem=got.at[phase],
            device_id=(row, col), device_id_type=MESH,
        ).start()

    def local(src, dst, phase):
        pltpu.make_async_copy(src, dst, got.at[phase]).start()

    def wait(sem, ref):
        pltpu.make_async_copy(ref, ref, sem).wait()

    def rows_of(ref, start, size, cols=None):
        at = pl.ds(pl.multiple_of(start, 8), size)
        if cols is None:
            return ref.at[at]
        return ref.at[at, pl.ds(cols[0], cols[1])]

    def lead_piece(ref, block, m):
        if block == 0:
            return rows_of(ref, m * 8, 8, (0, 512))
        if block == 1:
            return rows_of(ref, 512 + m * 8, 8, (0, 256))
        if block == 2:
            return rows_of(ref, 512 + m * 8, 8, (256, 256))
        return rows_of(ref, 512 + m * 8, 8, (512, 512))

    def summed_piece(block, m):
        if block == 1:
            return rows_of(summed, m * 8, 8, (0, 256))
        if block == 2:
            return rows_of(summed, m * 8, 8, (256, 256))
        return rows_of(summed, m * 8, 8, (0, 512))

    for owner_row, owner_col, blocks in ((0, 0, (0,)), (1, 0, (1, 2)), (1, 1, (3,))):
        @pl.when((my_row == owner_row) & (my_col == owner_col))
        def _():
            for block in blocks:
                target_core = 0 if block < 2 else 1

                @pl.loop(0, 64)
                def _(m):
                    row, col = m // 4, (m % 4) * 2 + target_core
                    here = (row == owner_row) & (col == owner_col)

                    @pl.when(here)
                    def _():
                        local(summed_piece(block, m), lead_piece(lead_ref, block, m), 0)

                    @pl.when(jnp.logical_not(here))
                    def _():
                        remote(
                            summed_piece(block, m), lead_piece(lead_ref, block, m), 0, row, col,
                            11 if block == 2 else 0,
                        )

    for src in range(2):
        @pl.when(my_col == src)
        def _():
            for k in range(4):
                piece = rows_of(summed, k * 256, 256, (0, 512))
                place = rows_of(rows_ref, k * 256, 256, (src * 512, 512))
                if k == 0:
                    local(piece, place, 2)
                else:
                    remote(piece, place, 2, my_row, 2 * k + src)

    @pl.loop(early, 4)
    def _(n):
        add_children(n)

    def scatter_rows(phase, start):
        for src in range(2):
            @pl.when(my_row == src)
            def _():
                for k in range(16):
                    piece = rows_of(summed, k * 32, 32, (start, 1024))
                    place = rows_of(cols_ref, src * NB + k * 32, 32, (start, 1024))
                    if k == src:
                        local(piece, place, phase)
                    else:
                        remote(piece, place, phase, k, my_col)

    scatter_rows(1, 0)

    @pl.when(core == 0)
    def _():
        wait(got.at[0], wait_bytes.at[pl.ds(0, 8), pl.ds(0, 768)])

        @pl.loop(1, 64)
        def _(t):
            other = lax.rem(chip + t, 64)
            for block in (0, 1):
                remote(lead_piece(lead_ref, block, chip), lead_piece(lead_ref, block, chip), 3, other // 4, (other % 4) * 2)

    @pl.when(core == 1)
    def _():
        wait(got.at[0], wait_bytes.at[pl.ds(0, 8), pl.ds(0, 768)])

        @pl.loop(1, 64)
        def _(t):
            other = lax.rem(chip + t, 64)
            for block in (2, 3):
                remote(lead_piece(lead_ref, block, chip), lead_piece(lead_ref, block, chip), 3, other // 4, (other % 4) * 2 + 1)

    wait(got.at[2], rows_of(wait_bytes, 0, 256, (0, 512)))
    for core_is in range(2):
        @pl.when(core == core_is)
        def _():
            for t in range(1, 4):
                piece = rows_of(rows_ref, x * 256, 256, (core_is * 512, 512))
                remote(piece, piece, 4, my_row, lax.rem(x + t, 4) * 2 + core_is)

    @pl.loop(4, 8)
    def _(n):
        add_children(n)

    scatter_rows(12, 1024)

    pltpu.make_async_copy(summed, summed_out, out_sems.at[4]).start()

    wait(got.at[3], rows_of(wait_bytes, 0, 504, (0, 768)))
    for core_is in range(2):
        @pl.when(core == core_is)
        def _():
            if core_is == 0:
                pieces = [lead_ref.at[pl.ds(0, 512), pl.ds(0, 512)], lead_ref.at[pl.ds(512, 512), pl.ds(0, 256)]]
            else:
                pieces = [lead_ref.at[pl.ds(512, 512), pl.ds(256, 256)], lead_ref.at[pl.ds(512, 512), pl.ds(512, 512)]]
            for piece in pieces:
                remote(piece, piece, 7, my_row, x * 2 + 1 - core_is)

    def first_left():
        wait(got.at[1], rows_of(wait_bytes, 0, 64, (0, 1024)))
        for src in range(2):
            left = rows_of(cols_ref, src * NB + my_row * 32, 32, (0, 1024))
            for t in range(1, 4):
                remote(left, left, 5, y * 4 + lax.rem(z + t, 4), my_col)

    def first_right():
        wait(got.at[12], rows_of(wait_bytes, 0, 64, (0, 1024)))
        for src in range(2):
            right = rows_of(cols_ref, src * NB + my_row * 32, 32, (1024, 1024))
            for t in range(1, 4):
                remote(right, right, 6, lax.rem(y + t, 4) * 4 + z, my_col)

    def second_left():
        wait(got.at[5], rows_of(wait_bytes, 0, 192, (0, 1024)))
        for src in range(2):
            left = rows_of(cols_ref, src * NB + y * 128, 128, (0, 1024))
            for t in range(1, 4):
                remote(left, left, 8, lax.rem(y + t, 4) * 4 + z, my_col)

    def second_right():
        wait(got.at[6], rows_of(wait_bytes, 0, 192, (0, 1024)))
        for src in range(2):
            for k in range(4):
                right = rows_of(cols_ref, src * NB + k * 128 + z * 32, 32, (1024, 1024))
                for t in range(1, 4):
                    remote(right, right, 9, y * 4 + lax.rem(z + t, 4), my_col)

    def other_core():
        wait(got.at[4], rows_of(wait_bytes, 0, 768, (0, 512)))
        for core_is in range(2):
            @pl.when(core == core_is)
            def _():
                piece = rows_ref.at[:, pl.ds(core_is * 512, 512)]
                remote(piece, piece, 10, my_row, x * 2 + 1 - core_is)

    first_left()
    wait(got.at[7], rows_of(wait_bytes, 0, 512, (0, 768)))
    factor_leading(
        lead_ref, lower, inverse, staged, corner,
        {0: first_right, 1: second_left, 2: second_right, 3: other_core},
    )
    pltpu.make_async_copy(
        grouped.at[:, :, pl.ds(0, 896)], grouped.at[:, :, pl.ds(0, 896)], send_sems.at[0]
    ).wait()
    pltpu.make_async_copy(
        grouped.at[:, pl.ds(0, 480), pl.ds(0, 128)],
        grouped.at[:, pl.ds(0, 480), pl.ds(0, 128)],
        send_sems.at[1],
    ).wait()

    for n in range(4):
        at = slice(n * 256, n * 256 + 256)
        stacked[0, at, :], stacked[1, at, :] = split2(inverse[at, :])
    outs = [
        pltpu.make_async_copy(stacked, inverse_out, out_sems.at[0]),
        pltpu.make_async_copy(grouped, factor_out, out_sems.at[1]),
        pltpu.make_async_copy(cols_ref.at[:, pl.ds(1024, 1024)], right_out, out_sems.at[2]),
        pltpu.make_async_copy(row_maps, left_out, out_sems.at[3]),
    ]
    outs[0].start()
    wait(got.at[10], rows_of(wait_bytes, 0, 1024, (0, 512)))
    for m in range(4):
        parts = split2(rows_ref[m * 256:m * 256 + 256, :])
        for n in range(4):
            past = slice(0, n * 256 + 256)
            here = slice(n * 256, n * 256 + 256)
            grouped[m // 2, m % 2 * 256:m % 2 * 256 + 256, here] = product(
                [part[:, past] for part in parts],
                (stacked[0, here, past], stacked[1, here, past]),
                ((1,), (1,)),
            )
    for src in range(2):
        @pl.when(my_row == src)
        def _():
            grouped[0] = lower[src * NB:src * NB + NB, :]
    outs[1].start()
    wait(got.at[8], rows_of(wait_bytes, 0, 768, (0, 1024)))
    for q in range(2):
        strip = slice(q * NB, q * NB + NB)
        for n in range(4):
            at = slice(n * 256, n * 256 + 256)
            col_hi[at, :], col_lo[at, :] = split2(cols_ref[at, strip])
        for n in range(4):
            past = slice(0, n * 256 + 256)
            here = slice(n * 256, n * 256 + 256)
            value = product(
                (stacked[0, here, past], stacked[1, here, past]),
                (col_hi[past, :], col_lo[past, :]),
                ((1,), (0,)),
            )
            row_maps[0, here, strip], row_maps[1, here, strip] = split2(value)
    outs[3].start()
    wait(got.at[9], rows_of(wait_bytes, 0, 768, (0, 1024)))
    outs[2].start()

    @pl.when((my_row == 0) & (my_col == 0))
    def _():
        wait(sent.at[0], rows_of(wait_bytes, 0, 504, (0, 512)))

    @pl.when((my_row == 1) & (my_col == 0))
    def _():
        wait(sent.at[0], rows_of(wait_bytes, 0, 504, (0, 256)))
        wait(sent.at[11], rows_of(wait_bytes, 0, 512, (0, 256)))

    @pl.when((my_row == 1) & (my_col == 1))
    def _():
        wait(sent.at[0], rows_of(wait_bytes, 0, 504, (0, 512)))

    @pl.when(my_row < 2)
    def _():
        wait(sent.at[1], rows_of(wait_bytes, 0, 480, (0, 1024)))
        wait(sent.at[12], rows_of(wait_bytes, 0, 480, (0, 1024)))

    @pl.when(my_col < 2)
    def _():
        wait(sent.at[2], rows_of(wait_bytes, 0, 768, (0, 512)))

    wait(sent.at[3], rows_of(wait_bytes, 0, 504, (0, 768)))
    wait(sent.at[4], rows_of(wait_bytes, 0, 768, (0, 512)))
    wait(sent.at[5], rows_of(wait_bytes, 0, 192, (0, 1024)))
    wait(sent.at[6], rows_of(wait_bytes, 0, 192, (0, 1024)))
    wait(sent.at[7], rows_of(wait_bytes, 0, 512, (0, 768)))
    wait(sent.at[8], rows_of(wait_bytes, 0, 768, (0, 1024)))
    wait(sent.at[9], rows_of(wait_bytes, 0, 768, (0, 1024)))
    wait(sent.at[10], rows_of(wait_bytes, 0, 1024, (0, 512)))
    for out in outs:
        out.wait()

    pltpu.make_async_copy(summed, summed_out, out_sems.at[4]).wait()


def local_position(ids, count):
    return ids // (NB * count) * NB + ids % NB


def id_tables(index_maps, rows, cols):
    my_row = lax.axis_index("row")
    my_col = lax.axis_index("col")
    ratio = rows // cols
    row_ids = lax.dynamic_index_in_dim(
        index_maps.reshape(2, rows, rows, -1), my_row, 2, keepdims=False
    ).reshape(2, -1)
    col_ids = lax.dynamic_index_in_dim(
        index_maps.reshape(2, cols, ratio, ratio, cols, -1), my_col, 4, keepdims=False
    ).reshape(2, -1)
    return local_position(row_ids, rows), local_position(col_ids, cols)[:, :, None]


def assemble(front, child_blocks, index_maps, rows, cols):
    row_ids, col_ids = id_tables(index_maps, rows, cols)
    vm = pl.BlockSpec(memory_space=pltpu.VMEM)
    anyspace = pl.BlockSpec(memory_space=pl.ANY)
    dma = pltpu.SemaphoreType.DMA
    return pl.pallas_call(
        functools.partial(front_kernel, rows, cols),
        out_shape=(
            jax.ShapeDtypeStruct((1024, 2048), F32),
            jax.ShapeDtypeStruct((2, NB, 1024), F32),
            jax.ShapeDtypeStruct((2, 1024, 1024), BF),
            jax.ShapeDtypeStruct((1024, 1024), F32),
            jax.ShapeDtypeStruct((2, 1024, 1024), BF),
        ),
        in_specs=[anyspace, anyspace, vm, vm],
        out_specs=[anyspace] * 5,
        scratch_shapes=[
            VM((1024, 1024), F32),
            VM((2, 512, 1024), F32),
            VM((2, 512, 1024), F32),
            VM((1024, 2048), F32),
            VM((2, 1024, 1024), BF),
            VM((2, 1024, 1024), BF),
            VM((1024, 1024), F32),
            VM((1024, 2048), F32),
            VM((1024, 1024), F32),
            VM((1024, 1024), F32),
            VM((1024, 1024), F32),
            VM((128, 128), F32),
            VM((1024, NB), BF),
            VM((1024, NB), BF),
            dma,
            dma((8,)),
            dma((2,)),
            dma,
            dma((13,)),
            dma((13,)),
            dma((5,)),
        ],
        compiler_params=pltpu.CompilerParams(vmem_limit_bytes=62 << 20, has_side_effects=True),
    )(child_blocks, front, row_ids, col_ids)


def update_kernel(summed_hbm, solved_hbm, inverse_hbm, right_hbm, left_hbm, schur_hbm, factor_hbm,
                  summed, solved, inverse, right, left, sol_hi, sol_lo,
                  col_hi, col_lo, y_hi, y_lo, in_sems, strip_sems, out_sems, factor_sems):
    loads = [
        pltpu.make_async_copy(solved_hbm.at[b], solved.at[pl.ds(b * NB, NB)], factor_sems.at[2 + b])
        for b in range(2)
    ]
    for load in loads:
        load.start()
    left_load = pltpu.make_async_copy(left_hbm, left, in_sems.at[0])
    left_load.start()

    def strip_load(q):
        at = pl.ds(q * NB, NB)
        return pltpu.make_async_copy(summed_hbm.at[:, at], summed.at[:, at], strip_sems.at[q])

    for q in range(2):
        strip_load(q).start()
    late = [
        pltpu.make_async_copy(inverse_hbm, inverse, in_sems.at[1]),
        pltpu.make_async_copy(right_hbm, right, in_sems.at[2]),
    ]
    for load in late:
        load.start()
    for q in range(2, 4):
        strip_load(q).start()

    stores = []
    for b in range(2):
        loads[b].wait()
        store = pltpu.make_async_copy(solved.at[pl.ds(b * NB, NB)], factor_hbm.at[b], factor_sems.at[b])
        store.start()
        stores.append(store)
        for r in range(2):
            at = slice(b * NB + r * 256, b * NB + r * 256 + 256)
            sol_hi[at, :], sol_lo[at, :] = split2(solved[at, :])
    left_load.wait()

    for q in range(4):
        strip = slice(q * NB, q * NB + NB)
        if q < 2:
            factors = (left.at[0, :, pl.ds(q * NB, NB)], left.at[1, :, pl.ds(q * NB, NB)])
        else:
            if q == 2:
                for load in late:
                    load.wait()
            source = slice((q - 2) * NB, (q - 1) * NB)
            for n in range(4):
                at = slice(n * 256, n * 256 + 256)
                col_hi[at, :], col_lo[at, :] = split2(right[at, source])
            for n in range(4):
                past = slice(0, n * 256 + 256)
                here = slice(n * 256, n * 256 + 256)
                value = product(
                    (inverse[0, here, past], inverse[1, here, past]),
                    (col_hi[past, :], col_lo[past, :]),
                    ((1,), (0,)),
                )
                y_hi[here, :], y_lo[here, :] = split2(value)
            factors = (y_hi, y_lo)
        strip_load(q).wait()

        @pl.loop(0, 4)
        def _(m):
            at = pl.ds(pl.multiple_of(m * 256, 256), 256)
            summed[at, strip] -= product(
                (sol_hi[at, :], sol_lo[at, :]), (factors[0][...], factors[1][...]), ((1,), (0,))
            )

        for b in range(2):
            store = pltpu.make_async_copy(
                summed.at[pl.ds(b * NB, NB), pl.ds(q * NB, NB)], schur_hbm.at[b, :, q, :], out_sems.at[2 * q + b]
            )
            store.start()
            stores.append(store)
    for store in stores:
        store.wait()


def update(*parts):
    anyspace = pl.BlockSpec(memory_space=pl.ANY)
    return pl.pallas_call(
        update_kernel,
        out_shape=(
            jax.ShapeDtypeStruct((2, NB, 4, NB), F32),
            jax.ShapeDtypeStruct((2, NB, 2 * NB), F32),
        ),
        in_specs=[anyspace] * 5,
        out_specs=[anyspace] * 2,
        scratch_shapes=[
            VM((1024, 2048), F32),
            VM((1024, 1024), F32),
            VM((2, 1024, 1024), BF),
            VM((1024, 1024), F32),
            VM((2, 1024, 1024), BF),
            VM((1024, 1024), BF),
            VM((1024, 1024), BF),
            VM((1024, NB), BF),
            VM((1024, NB), BF),
            VM((1024, NB), BF),
            VM((1024, NB), BF),
            pltpu.SemaphoreType.DMA((3,)),
            pltpu.SemaphoreType.DMA((4,)),
            pltpu.SemaphoreType.DMA((8,)),
            pltpu.SemaphoreType.DMA((4,)),
        ],
        compiler_params=pltpu.CompilerParams(vmem_limit_bytes=60 << 20),
    )(*parts)


def on_device(front, child_blocks, index_maps):
    parts = assemble(front, child_blocks, index_maps, lax.axis_size("row"), lax.axis_size("col"))
    return update(*parts)


def solution(mesh):
    placed = (P(None, "row", None, "col"), P(None, "row", "col"), P())
    return jax.shard_map(
        on_device,
        mesh=mesh,
        in_specs=placed,
        out_specs=(P(None, "row", None, "col"), P(None, "row", None)),
        check_vma=False,
    )
```

```python
import functools

import jax
import jax.numpy as jnp
from jax import lax
from jax.experimental import pallas as pl
from jax.experimental.pallas import tpu as pltpu
from jax.sharding import PartitionSpec as P

NB = 512
MESH = pl.DeviceIdType.MESH
BF = jnp.bfloat16
F32 = jnp.float32
VM = pltpu.VMEM
HI = lax.Precision.HIGHEST


def split2(value):
    first = value.astype(BF)
    return first, (value - first.astype(F32)).astype(BF)


def product(left, right, dims):
    parts = [(0, 0), (0, 1), (1, 0)]
    total = None
    for a, b in parts:
        term = lax.dot_general(left[a], right[b], (dims, ((), ())), preferred_element_type=F32)
        total = term if total is None else total + term
    return total


def dot(left, right):
    return jnp.dot(left, right, preferred_element_type=F32)


def dot_nn(a,b): return lax.dot_general(a,b,(((1,),(0,)),((),())),precision=HI,preferred_element_type=F32)
def dot_nt(a,b): return lax.dot_general(a,b,(((1,),(1,)),((),())),precision=HI,preferred_element_type=F32)

def inverse_factor(block):
    n, group = 128, 8
    full = (8, n)
    lane = lax.broadcasted_iota(jnp.int32, full, 1)
    sub = lax.broadcasted_iota(jnp.int32, full, 0)
    tiles = [block[8 * i:8 * i + 8, :] for i in range(n // 8)]
    for at in range(n // 8):
        j = at * group
        inside = (lane >= j) & (lane < j + group)
        first = [jnp.broadcast_to(tiles[at][:, j + a:j + a + 1], full) for a in range(group)]
        pivots = [
            [jnp.broadcast_to(first[a][b:b + 1, :], full) for a in range(b + 1)] for b in range(group)
        ]
        solved = []
        for a in range(group):
            row = jnp.broadcast_to(tiles[at][a:a + 1, :], full)
            solved.append(jnp.where(lane == j + a, 1.0, jnp.where(inside, 0.0, row)))
        factors = [[None] * group for _ in range(group)]
        inverses = [None] * group
        for a in range(group):
            inverses[a] = 1.0 / pivots[a][a]
            for b in range(a + 1, group):
                factors[b][a] = pivots[b][a] * inverses[a]
            for b in range(a + 1, group):
                for c in range(a + 1, b + 1):
                    pivots[b][c] = pivots[b][c] - factors[b][a] * pivots[c][a]
                solved[b] = solved[b] - factors[b][a] * solved[a]
        lines = [inverses[b] * solved[b] for b in range(group)]
        for a in range(group - 2, -1, -1):
            for b in range(a + 1, group):
                lines[a] = lines[a] - factors[b][a] * lines[b]
        made = tiles[at]
        for b in range(group):
            made = jnp.where(sub == b, jnp.where(lane == j + b, pivots[b][b], solved[b]), made)
        tiles[at] = made
        for i in range(at + 1, n // 8):
            value = jnp.where(inside, 0.0, tiles[i])
            for a in range(group):
                value = value - jnp.broadcast_to(tiles[i][:, j + a:j + a + 1], full) * lines[a]
            tiles[i] = value
    whole = jnp.concatenate(tiles, axis=0)
    r = lax.broadcasted_iota(jnp.int32, (n, n), 0)
    c = lax.broadcasted_iota(jnp.int32, (n, n), 1)
    diag = jnp.sum(jnp.where(r == c, whole, 0.0), axis=1, keepdims=True)
    unit = jnp.where(r > c, whole, jnp.where(r == c, 1.0, 0.0))
    return unit * (1.0 / jnp.sqrt(diag))


def factor_leading(lead, lower, inverse, work, corner, between):
    n = 128
    r = lax.broadcasted_iota(jnp.int32, (n, n), 0)
    c = lax.broadcasted_iota(jnp.int32, (n, n), 1)
    work[...] = lead[...]
    lower[...] = jnp.zeros_like(lower)
    inverse[...] = jnp.zeros_like(inverse)

    @pl.loop(0, 8)
    def _(j):
        at = pl.ds(pl.multiple_of(j * n, n), n)
        corner[...] = inverse_factor(work[at, at])
        for s in range(8):
            @pl.when(j == s)
            def _():
                at = slice(s * n, s * n + n)
                w = corner[...]
                lower[at, at] = jnp.where(r >= c, dot_nt(work[at, at], w), 0.0)
                inverse[at, at] = w
                if s < 7:
                    p = dot_nt(work[s * n + n:, at], w)
                    lower[s * n + n:, at] = p
                    for k in range(s + 1, 8):
                        o = (k - s - 1) * n
                        work[k * n:, k * n:k * n + n] -= dot_nt(p[o:], p[o:o + n])
                if s:
                    done = slice(0, s * n)
                    inverse[at, done] = -dot_nn(w, dot_nn(lower[at, done], inverse[done, done]))
                if s in between:
                    between[s]()


def front_kernel(rows, cols, child_ref, front_ref, row_ids_ref, col_ids_ref,
                 summed_out, factor_out, inverse_out, right_out, left_out,
                 staged, grouped, received, summed, stacked, row_maps, rows_ref, cols_ref, lead_ref,
                 lower, inverse, corner, col_hi, col_lo, child_sem, front_sems, send_sems, recv_sem, sent, got, out_sems):
    my_row = lax.axis_index("row")
    my_col = lax.axis_index("col")
    y, z = my_row // 4, my_row % 4
    x, core = my_col // 2, my_col % 2
    chip = my_row * 4 + x
    wait_bytes = cols_ref
    for h in range(2):
        pltpu.make_async_copy(child_ref.at[h], staged.at[pl.ds(h * NB, NB)], child_sem).start()
    for b in range(2):
        for q in range(4):
            pltpu.make_async_copy(
                front_ref.at[b, :, q, :],
                summed.at[pl.ds(b * NB, NB), pl.ds(q * NB, NB)],
                front_sems.at[b * 4 + q],
            ).start()
    pltpu.make_async_copy(staged, staged, child_sem).wait()

    def group_rows(k):
        lanes = lax.broadcasted_iota(jnp.int32, (32, 128), 1) // 32
        at = pl.ds(pl.multiple_of(k * 32, 32), 32)
        for h in range(2):
            source_at = pl.ds(pl.multiple_of(h * NB + k * 32, 32), 32)
            tiles = [staged[source_at, t * 128:(t + 1) * 128] for t in range(8)]
            for dest in range(8):
                made = None
                for part in range(4):
                    source = tiles[part * 2 + dest // 4]
                    shift = (part * 32 - (dest % 4) * 32) % 128
                    moved = pltpu.roll(source, shift, axis=1) if shift else source
                    made = moved if made is None else jnp.where(lanes == part, moved, made)
                grouped[h, at, dest * 128:(dest + 1) * 128] = made

    def block(ref, row, col):
        return ref.at[
            :, pl.ds(pl.multiple_of(row * 32, 32), 32), pl.ds(pl.multiple_of(col * 128, 128), 128)
        ]

    def send(k, dest, sem):
        pltpu.make_async_remote_copy(
            src_ref=block(grouped, k, dest),
            dst_ref=block(received, my_row, my_col),
            send_sem=send_sems.at[sem],
            recv_sem=recv_sem,
            device_id=(k, dest),
            device_id_type=MESH,
        ).start()

    @pl.loop(0, rows)
    def _(t):
        k = lax.rem(my_row + t * 5, rows)
        group_rows(k)
        for u in range(1, cols):
            send(k, lax.rem(my_col + u, cols), 0)

        @pl.when(t > 0)
        def _():
            send(k, my_col, 1)

    own = pltpu.make_async_copy(
        block(grouped, my_row, my_col), block(received, my_row, my_col), recv_sem
    )
    own.start()
    for b in range(2):
        for q in range(4):
            pltpu.make_async_copy(
                front_ref.at[b, :, q, :],
                summed.at[pl.ds(b * NB, NB), pl.ds(q * NB, NB)],
                front_sems.at[b * 4 + q],
            ).wait()
    for h in range(2):
        chosen = (
            lax.broadcasted_iota(jnp.int32, (1024, 512), 0) == row_ids_ref[h:h + 1, :]
        ).astype(BF)
        row_maps[h, :, 0:512] = chosen
        row_maps[h, :, 512:1024] = chosen
    pltpu.make_async_copy(received, received, recv_sem).wait()
    for h in range(2):
        for r in (0, 256):
            stacked[h, r:r + 256, :], stacked[h, 512 + r:768 + r, :] = split2(received[h, r:r + 256, :])

    def add_children(n):
        at = pl.ds(pl.multiple_of(n * 256, 256), 256)
        total = summed[:, at]
        for h in range(2):
            col_map = (
                lax.broadcasted_iota(jnp.int32, (1024, 256), 1) + n * 256 == col_ids_ref[h]
            ).astype(BF)
            total += dot(row_maps[h], dot(stacked[h], col_map).astype(BF))
        summed[:, at] = total

    early = jnp.where(my_col < 2, 2, 0)

    @pl.loop(0, early)
    def _(n):
        add_children(n)

    def remote(src, dst, phase, row, col, send_phase=None):
        leaving = sent.at[phase if send_phase is None else send_phase]
        pltpu.make_async_remote_copy(
            src_ref=src, dst_ref=dst, send_sem=leaving, recv_sem=got.at[phase],
            device_id=(row, col), device_id_type=MESH,
        ).start()

    def local(src, dst, phase):
        pltpu.make_async_copy(src, dst, got.at[phase]).start()

    def wait(sem, ref):
        pltpu.make_async_copy(ref, ref, sem).wait()

    def rows_of(ref, start, size, cols=None):
        at = pl.ds(pl.multiple_of(start, 8), size)
        if cols is None:
            return ref.at[at]
        return ref.at[at, pl.ds(cols[0], cols[1])]

    def lead_piece(ref, block, m):
        if block == 0:
            return rows_of(ref, m * 8, 8, (0, 512))
        if block == 1:
            return rows_of(ref, 512 + m * 8, 8, (0, 256))
        if block == 2:
            return rows_of(ref, 512 + m * 8, 8, (256, 256))
        return rows_of(ref, 512 + m * 8, 8, (512, 512))

    def summed_piece(block, m):
        if block == 1:
            return rows_of(summed, m * 8, 8, (0, 256))
        if block == 2:
            return rows_of(summed, m * 8, 8, (256, 256))
        return rows_of(summed, m * 8, 8, (0, 512))

    for owner_row, owner_col, blocks in ((0, 0, (0,)), (1, 0, (1, 2)), (1, 1, (3,))):
        @pl.when((my_row == owner_row) & (my_col == owner_col))
        def _():
            for block in blocks:
                target_core = 0 if block < 2 else 1

                @pl.loop(0, 64)
                def _(m):
                    row, col = m // 4, (m % 4) * 2 + target_core
                    here = (row == owner_row) & (col == owner_col)

                    @pl.when(here)
                    def _():
                        local(summed_piece(block, m), lead_piece(lead_ref, block, m), 0)

                    @pl.when(jnp.logical_not(here))
                    def _():
                        remote(
                            summed_piece(block, m), lead_piece(lead_ref, block, m), 0, row, col,
                            11 if block == 2 else 0,
                        )

    for src in range(2):
        @pl.when(my_col == src)
        def _():
            for k in range(4):
                piece = rows_of(summed, k * 256, 256, (0, 512))
                place = rows_of(rows_ref, k * 256, 256, (src * 512, 512))
                if k == 0:
                    local(piece, place, 2)
                else:
                    remote(piece, place, 2, my_row, 2 * k + src)

    @pl.loop(early, 4)
    def _(n):
        add_children(n)

    def scatter_rows(phase, start):
        for src in range(2):
            @pl.when(my_row == src)
            def _():
                for t in range(16):
                    k = (t * 5 + src) % 16
                    piece = rows_of(summed, k * 32, 32, (start, 1024))
                    place = rows_of(cols_ref, src * NB + k * 32, 32, (start, 1024))
                    if k == src:
                        local(piece, place, phase)
                    else:
                        remote(piece, place, phase, k, my_col)

    scatter_rows(1, 0)

    @pl.when(core == 0)
    def _():
        wait(got.at[0], wait_bytes.at[pl.ds(0, 8), pl.ds(0, 768)])

        @pl.loop(1, 64)
        def _(t):
            other = lax.rem(chip + t * 13, 64)
            for block in (0, 1):
                remote(lead_piece(lead_ref, block, chip), lead_piece(lead_ref, block, chip), 3, other // 4, (other % 4) * 2)

    @pl.when(core == 1)
    def _():
        wait(got.at[0], wait_bytes.at[pl.ds(0, 8), pl.ds(0, 768)])

        @pl.loop(1, 64)
        def _(t):
            other = lax.rem(chip + t * 13, 64)
            for block in (2, 3):
                remote(lead_piece(lead_ref, block, chip), lead_piece(lead_ref, block, chip), 3, other // 4, (other % 4) * 2 + 1)

    wait(got.at[2], rows_of(wait_bytes, 0, 256, (0, 512)))
    for core_is in range(2):
        @pl.when(core == core_is)
        def _():
            for t in range(1, 4):
                piece = rows_of(rows_ref, x * 256, 256, (core_is * 512, 512))
                remote(piece, piece, 4, my_row, lax.rem(x + t, 4) * 2 + core_is)

    @pl.loop(4, 8)
    def _(n):
        add_children(n)

    scatter_rows(12, 1024)

    pltpu.make_async_copy(summed, summed_out, out_sems.at[4]).start()

    wait(got.at[3], rows_of(wait_bytes, 0, 504, (0, 768)))
    for core_is in range(2):
        @pl.when(core == core_is)
        def _():
            if core_is == 0:
                pieces = [lead_ref.at[pl.ds(0, 512), pl.ds(0, 512)], lead_ref.at[pl.ds(512, 512), pl.ds(0, 256)]]
            else:
                pieces = [lead_ref.at[pl.ds(512, 512), pl.ds(256, 256)], lead_ref.at[pl.ds(512, 512), pl.ds(512, 512)]]
            for piece in pieces:
                remote(piece, piece, 7, my_row, x * 2 + 1 - core_is)

    def first_left():
        wait(got.at[1], rows_of(wait_bytes, 0, 64, (0, 1024)))
        for src in range(2):
            left = rows_of(cols_ref, src * NB + my_row * 32, 32, (0, 1024))
            for t in range(1, 4):
                remote(left, left, 5, y * 4 + lax.rem(z + t, 4), my_col)

    def first_right():
        wait(got.at[12], rows_of(wait_bytes, 0, 64, (0, 1024)))
        for src in range(2):
            right = rows_of(cols_ref, src * NB + my_row * 32, 32, (1024, 1024))
            for t in range(1, 4):
                remote(right, right, 6, lax.rem(y + t, 4) * 4 + z, my_col)

    def second_left():
        wait(got.at[5], rows_of(wait_bytes, 0, 192, (0, 1024)))
        for src in range(2):
            left = rows_of(cols_ref, src * NB + y * 128, 128, (0, 1024))
            for t in range(1, 4):
                remote(left, left, 8, lax.rem(y + t, 4) * 4 + z, my_col)

    def second_right():
        wait(got.at[6], rows_of(wait_bytes, 0, 192, (0, 1024)))
        for src in range(2):
            for k in range(4):
                right = rows_of(cols_ref, src * NB + k * 128 + z * 32, 32, (1024, 1024))
                for t in range(1, 4):
                    remote(right, right, 9, y * 4 + lax.rem(z + t, 4), my_col)

    def other_core():
        wait(got.at[4], rows_of(wait_bytes, 0, 768, (0, 512)))
        for core_is in range(2):
            @pl.when(core == core_is)
            def _():
                piece = rows_ref.at[:, pl.ds(core_is * 512, 512)]
                remote(piece, piece, 10, my_row, x * 2 + 1 - core_is)

    first_left()
    wait(got.at[7], rows_of(wait_bytes, 0, 512, (0, 768)))
    factor_leading(
        lead_ref, lower, inverse, staged, corner,
        {0: first_right, 1: second_left, 2: second_right, 3: other_core},
    )
    pltpu.make_async_copy(
        grouped.at[:, :, pl.ds(0, 896)], grouped.at[:, :, pl.ds(0, 896)], send_sems.at[0]
    ).wait()
    pltpu.make_async_copy(
        grouped.at[:, pl.ds(0, 480), pl.ds(0, 128)],
        grouped.at[:, pl.ds(0, 480), pl.ds(0, 128)],
        send_sems.at[1],
    ).wait()

    for n in range(4):
        at = slice(n * 256, n * 256 + 256)
        stacked[0, at, :], stacked[1, at, :] = split2(inverse[at, :])
    outs = [
        pltpu.make_async_copy(stacked, inverse_out, out_sems.at[0]),
        pltpu.make_async_copy(grouped, factor_out, out_sems.at[1]),
        pltpu.make_async_copy(cols_ref.at[:, pl.ds(1024, 1024)], right_out, out_sems.at[2]),
        pltpu.make_async_copy(row_maps, left_out, out_sems.at[3]),
    ]
    outs[0].start()
    wait(got.at[10], rows_of(wait_bytes, 0, 1024, (0, 512)))
    for m in range(4):
        parts = split2(rows_ref[m * 256:m * 256 + 256, :])
        for n in range(4):
            past = slice(0, n * 256 + 256)
            here = slice(n * 256, n * 256 + 256)
            grouped[m // 2, m % 2 * 256:m % 2 * 256 + 256, here] = product(
                [part[:, past] for part in parts],
                (stacked[0, here, past], stacked[1, here, past]),
                ((1,), (1,)),
            )
    for src in range(2):
        @pl.when(my_row == src)
        def _():
            grouped[0] = lower[src * NB:src * NB + NB, :]
    outs[1].start()
    wait(got.at[8], rows_of(wait_bytes, 0, 768, (0, 1024)))
    for q in range(2):
        strip = slice(q * NB, q * NB + NB)
        for n in range(4):
            at = slice(n * 256, n * 256 + 256)
            col_hi[at, :], col_lo[at, :] = split2(cols_ref[at, strip])
        for n in range(4):
            past = slice(0, n * 256 + 256)
            here = slice(n * 256, n * 256 + 256)
            value = product(
                (stacked[0, here, past], stacked[1, here, past]),
                (col_hi[past, :], col_lo[past, :]),
                ((1,), (0,)),
            )
            row_maps[0, here, strip], row_maps[1, here, strip] = split2(value)
    outs[3].start()
    wait(got.at[9], rows_of(wait_bytes, 0, 768, (0, 1024)))
    outs[2].start()

    @pl.when((my_row == 0) & (my_col == 0))
    def _():
        wait(sent.at[0], rows_of(wait_bytes, 0, 504, (0, 512)))

    @pl.when((my_row == 1) & (my_col == 0))
    def _():
        wait(sent.at[0], rows_of(wait_bytes, 0, 504, (0, 256)))
        wait(sent.at[11], rows_of(wait_bytes, 0, 512, (0, 256)))

    @pl.when((my_row == 1) & (my_col == 1))
    def _():
        wait(sent.at[0], rows_of(wait_bytes, 0, 504, (0, 512)))

    @pl.when(my_row < 2)
    def _():
        wait(sent.at[1], rows_of(wait_bytes, 0, 480, (0, 1024)))
        wait(sent.at[12], rows_of(wait_bytes, 0, 480, (0, 1024)))

    @pl.when(my_col < 2)
    def _():
        wait(sent.at[2], rows_of(wait_bytes, 0, 768, (0, 512)))

    wait(sent.at[3], rows_of(wait_bytes, 0, 504, (0, 768)))
    wait(sent.at[4], rows_of(wait_bytes, 0, 768, (0, 512)))
    wait(sent.at[5], rows_of(wait_bytes, 0, 192, (0, 1024)))
    wait(sent.at[6], rows_of(wait_bytes, 0, 192, (0, 1024)))
    wait(sent.at[7], rows_of(wait_bytes, 0, 512, (0, 768)))
    wait(sent.at[8], rows_of(wait_bytes, 0, 768, (0, 1024)))
    wait(sent.at[9], rows_of(wait_bytes, 0, 768, (0, 1024)))
    wait(sent.at[10], rows_of(wait_bytes, 0, 1024, (0, 512)))
    for out in outs:
        out.wait()

    pltpu.make_async_copy(summed, summed_out, out_sems.at[4]).wait()


def local_position(ids, count):
    return ids // (NB * count) * NB + ids % NB


def id_tables(index_maps, rows, cols):
    my_row = lax.axis_index("row")
    my_col = lax.axis_index("col")
    ratio = rows // cols
    row_ids = lax.dynamic_index_in_dim(
        index_maps.reshape(2, rows, rows, -1), my_row, 2, keepdims=False
    ).reshape(2, -1)
    col_ids = lax.dynamic_index_in_dim(
        index_maps.reshape(2, cols, ratio, ratio, cols, -1), my_col, 4, keepdims=False
    ).reshape(2, -1)
    return local_position(row_ids, rows), local_position(col_ids, cols)[:, :, None]


def assemble(front, child_blocks, index_maps, rows, cols):
    row_ids, col_ids = id_tables(index_maps, rows, cols)
    vm = pl.BlockSpec(memory_space=pltpu.VMEM)
    anyspace = pl.BlockSpec(memory_space=pl.ANY)
    dma = pltpu.SemaphoreType.DMA
    return pl.pallas_call(
        functools.partial(front_kernel, rows, cols),
        out_shape=(
            jax.ShapeDtypeStruct((1024, 2048), F32),
            jax.ShapeDtypeStruct((2, NB, 1024), F32),
            jax.ShapeDtypeStruct((2, 1024, 1024), BF),
            jax.ShapeDtypeStruct((1024, 1024), F32),
            jax.ShapeDtypeStruct((2, 1024, 1024), BF),
        ),
        in_specs=[anyspace, anyspace, vm, vm],
        out_specs=[anyspace] * 5,
        scratch_shapes=[
            VM((1024, 1024), F32),
            VM((2, 512, 1024), F32),
            VM((2, 512, 1024), F32),
            VM((1024, 2048), F32),
            VM((2, 1024, 1024), BF),
            VM((2, 1024, 1024), BF),
            VM((1024, 1024), F32),
            VM((1024, 2048), F32),
            VM((1024, 1024), F32),
            VM((1024, 1024), F32),
            VM((1024, 1024), F32),
            VM((128, 128), F32),
            VM((1024, NB), BF),
            VM((1024, NB), BF),
            dma,
            dma((8,)),
            dma((2,)),
            dma,
            dma((13,)),
            dma((13,)),
            dma((5,)),
        ],
        compiler_params=pltpu.CompilerParams(vmem_limit_bytes=62 << 20, has_side_effects=True),
    )(child_blocks, front, row_ids, col_ids)


def update_kernel(summed_hbm, solved_hbm, inverse_hbm, right_hbm, left_hbm, schur_hbm, factor_hbm,
                  summed, solved, inverse, right, left, sol_hi, sol_lo,
                  col_hi, col_lo, y_hi, y_lo, in_sems, strip_sems, out_sems, factor_sems):
    loads = [
        pltpu.make_async_copy(solved_hbm.at[b], solved.at[pl.ds(b * NB, NB)], factor_sems.at[2 + b])
        for b in range(2)
    ]
    for load in loads:
        load.start()
    left_load = pltpu.make_async_copy(left_hbm, left, in_sems.at[0])
    left_load.start()

    def strip_load(q):
        at = pl.ds(q * NB, NB)
        return pltpu.make_async_copy(summed_hbm.at[:, at], summed.at[:, at], strip_sems.at[q])

    for q in range(2):
        strip_load(q).start()
    late = [
        pltpu.make_async_copy(inverse_hbm, inverse, in_sems.at[1]),
        pltpu.make_async_copy(right_hbm, right, in_sems.at[2]),
    ]
    for load in late:
        load.start()
    for q in range(2, 4):
        strip_load(q).start()

    stores = []
    for b in range(2):
        loads[b].wait()
        store = pltpu.make_async_copy(solved.at[pl.ds(b * NB, NB)], factor_hbm.at[b], factor_sems.at[b])
        store.start()
        stores.append(store)
        for r in range(2):
            at = slice(b * NB + r * 256, b * NB + r * 256 + 256)
            sol_hi[at, :], sol_lo[at, :] = split2(solved[at, :])
    left_load.wait()

    for q in range(4):
        strip = slice(q * NB, q * NB + NB)
        if q < 2:
            factors = (left.at[0, :, pl.ds(q * NB, NB)], left.at[1, :, pl.ds(q * NB, NB)])
        else:
            if q == 2:
                for load in late:
                    load.wait()
            source = slice((q - 2) * NB, (q - 1) * NB)
            for n in range(4):
                at = slice(n * 256, n * 256 + 256)
                col_hi[at, :], col_lo[at, :] = split2(right[at, source])
            for n in range(4):
                past = slice(0, n * 256 + 256)
                here = slice(n * 256, n * 256 + 256)
                value = product(
                    (inverse[0, here, past], inverse[1, here, past]),
                    (col_hi[past, :], col_lo[past, :]),
                    ((1,), (0,)),
                )
                y_hi[here, :], y_lo[here, :] = split2(value)
            factors = (y_hi, y_lo)
        strip_load(q).wait()

        @pl.loop(0, 4)
        def _(m):
            at = pl.ds(pl.multiple_of(m * 256, 256), 256)
            summed[at, strip] -= product(
                (sol_hi[at, :], sol_lo[at, :]), (factors[0][...], factors[1][...]), ((1,), (0,))
            )

        for b in range(2):
            store = pltpu.make_async_copy(
                summed.at[pl.ds(b * NB, NB), pl.ds(q * NB, NB)], schur_hbm.at[b, :, q, :], out_sems.at[2 * q + b]
            )
            store.start()
            stores.append(store)
    for store in stores:
        store.wait()


def update(*parts):
    anyspace = pl.BlockSpec(memory_space=pl.ANY)
    return pl.pallas_call(
        update_kernel,
        out_shape=(
            jax.ShapeDtypeStruct((2, NB, 4, NB), F32),
            jax.ShapeDtypeStruct((2, NB, 2 * NB), F32),
        ),
        in_specs=[anyspace] * 5,
        out_specs=[anyspace] * 2,
        scratch_shapes=[
            VM((1024, 2048), F32),
            VM((1024, 1024), F32),
            VM((2, 1024, 1024), BF),
            VM((1024, 1024), F32),
            VM((2, 1024, 1024), BF),
            VM((1024, 1024), BF),
            VM((1024, 1024), BF),
            VM((1024, NB), BF),
            VM((1024, NB), BF),
            VM((1024, NB), BF),
            VM((1024, NB), BF),
            pltpu.SemaphoreType.DMA((3,)),
            pltpu.SemaphoreType.DMA((4,)),
            pltpu.SemaphoreType.DMA((8,)),
            pltpu.SemaphoreType.DMA((4,)),
        ],
        compiler_params=pltpu.CompilerParams(vmem_limit_bytes=60 << 20),
    )(*parts)


def on_device(front, child_blocks, index_maps):
    parts = assemble(front, child_blocks, index_maps, lax.axis_size("row"), lax.axis_size("col"))
    return update(*parts)


def solution(mesh):
    placed = (P(None, "row", None, "col"), P(None, "row", "col"), P())
    return jax.shard_map(
        on_device,
        mesh=mesh,
        in_specs=placed,
        out_specs=(P(None, "row", None, "col"), P(None, "row", None)),
        check_vma=False,
    )
```
